128 devices in a mesh: pair: 8 (over z, core), tm: 16 (over y, x).
Axes of the slice: x: 4, y: 4, z: 4, core: 2. Of those that a mesh axis runs over, the one named last changes fastest.
Arguments:
- records: bfloat16 [512, 256, 2048], P('pair', 'tm'), may hold values from -60 to 60, as said below
- pair_list: int32 [1024, 2], replicated, may hold values from 0 to 511, as said below
- sketch: float32 [16, 2048], replicated, may hold values from -6 to 6
Outputs:
- stacks: float32 [1024, 2048], P('pair')
The draws below stay inside these ranges and needn't reach their ends.
Inputs may be any that keep to these rules, and one draw needn't show every extreme that they name: `pair_list`: rows p * 128 to (p + 1) * 128 - 1 name at most 12 distinct channels from any one block of channels o * 64 to (o + 1) * 64 - 1, and exactly 12 from one such block; the 256 channel slots of a pair index cycle through its listed channels, so each listed channel is used. `records`: each channel is a delayed copy of a field common to all channels plus its own noise, times a channel gain.
All inputs are finite; a program needn't handle non-finite values.
Results may differ from the reference program's by a relative error of at most 0.0041.
The reference program's roundings to bfloat16 on the way (of `white` and `cross`) count: a program that leaves them out, or rounds other values in their place, can miss the bound.
Values may be sent and summed in bfloat16 or wider, within the bound.
No kernel may reach another device: no remote copies, remote signals or barrier semaphores. Data moves between devices by JAX's collectives and lax.ppermute only.
A program may use at most 192 MiB of HBM per device.

```python
import math
import jax
import jax.numpy as jnp
from jax import lax

SAMPLES = 2048
NF = 512
LAGS = 2048
RANK = 16
CAP = 12
CH_DEV = 64
PAIRS_DEV = 128
CHANNELS = 512
WINDOWS = 256
PAIRS = 1024


def one_listing(key, n_pair):
    k_count, k_hot, k_perm, k_order = jax.random.split(key, 4)
    counts = jax.random.randint(k_count, (n_pair,), CAP // 4, CAP // 2 + 1)
    hot = jax.random.randint(k_hot, (), 0, n_pair)
    counts = jnp.where(jnp.arange(n_pair) == hot, CAP, counts)
    perms = jax.vmap(lambda k: jax.random.permutation(k, CH_DEV))(jax.random.split(k_perm, n_pair))
    chosen = (jnp.arange(n_pair)[:, None] * CH_DEV + perms[:, :CAP]).reshape(-1)
    valid = (jnp.arange(CAP)[None, :] < counts[:, None]).reshape(-1)
    order = jax.random.permutation(k_order, n_pair * CAP)
    score = jnp.where(valid, order, order + n_pair * CAP)
    listed = chosen[jnp.argsort(score, stable=True)]
    used = jnp.sum(counts)
    index = jnp.arange(PAIRS_DEV)
    first = listed[jnp.mod(2 * index, used)]
    second = listed[jnp.mod(2 * index + 1, used)]
    return jnp.stack([first, second], axis=1)


def draw_pair_list(key, part):
    n_pair = PAIRS // PAIRS_DEV
    keys = jax.random.split(jax.random.fold_in(key, 11), n_pair)
    blocks = jax.vmap(lambda k: one_listing(k, n_pair))(keys)
    return blocks.reshape(PAIRS, 2).astype(jnp.int32)


def draw_records(key, part):
    k_delay, k_field, k_noise, k_gain = jax.random.split(jax.random.fold_in(key, 23), 4)
    delays = jax.random.randint(k_delay, (CHANNELS,), 0, SAMPLES)
    field = jax.random.normal(k_field, (WINDOWS, SAMPLES), jnp.float32)
    gains = jnp.exp(jax.random.uniform(k_gain, (CHANNELS,), jnp.float32, math.log(0.3), math.log(3.0)))
    noise = jax.random.normal(k_noise, (CHANNELS, WINDOWS, SAMPLES), jnp.float32)
    strength = 0.5
    times = jnp.arange(SAMPLES).astype(jnp.int32)

    def shifted(delay):
        return jnp.take(field, jnp.mod(times - delay, SAMPLES), axis=1)
    common = lax.map(shifted, delays)
    values = gains[:, None, None] * (strength * common + noise)
    return jnp.clip(values, -60.0, 60.0).astype(jnp.bfloat16)


def centred(rng, dims, scale, most, kind=jnp.bfloat16):
    entries = jax.random.normal(rng, dims, jnp.float32) * scale
    return jnp.minimum(jnp.maximum(entries, -most), most).astype(kind)


def setup_inputs(seed: int = 0) -> dict:
    seeds = jax.random.split(jax.random.key(seed), 4)
    records = draw_records(jax.random.fold_in(seeds[3], 71), 0)
    pair_list = draw_pair_list(jax.random.fold_in(seeds[3], 71), 0)
    sketch = centred(seeds[2], (RANK, LAGS), 1.0, 6.0, jnp.float32)
    return {"records": records, "pair_list": pair_list, "sketch": sketch}


def tables():
    freq = (NF // 2 + jnp.arange(NF)).astype(jnp.int32)
    times = jnp.arange(SAMPLES).astype(jnp.int32)
    turn = jnp.mod(times[:, None] * freq[None, :], SAMPLES).astype(jnp.float32) * (2.0 * math.pi / SAMPLES)
    forward = jnp.concatenate([jnp.cos(turn), jnp.sin(turn)], axis=1).astype(jnp.bfloat16)
    shifts = (jnp.arange(LAGS) - LAGS // 2).astype(jnp.int32)
    angle = jnp.mod(freq[:, None] * shifts[None, :], SAMPLES).astype(jnp.float32) * (2.0 * math.pi / SAMPLES)
    inverse = (jnp.concatenate([jnp.cos(angle), -jnp.sin(angle)], axis=0) / math.sqrt(NF)).astype(jnp.bfloat16)
    return (forward, inverse)

def whiten(block, forward):
    spectra = jnp.dot(block.astype(jnp.float32), forward.astype(jnp.float32), preferred_element_type=jnp.float32)
    real_part = spectra[:, :NF]
    imag_part = spectra[:, NF:]
    power = real_part * real_part + imag_part * imag_part
    level = lax.optimization_barrier(jnp.mean(power, axis=1, keepdims=True))
    factor = lax.rsqrt(power + level + 1e-06)
    return jnp.concatenate([real_part * factor, imag_part * factor], axis=1).astype(jnp.bfloat16)

def correlate(first, second):
    left = first.astype(jnp.float32)
    right = second.astype(jnp.float32)
    lre, lim = (left[..., :NF], left[..., NF:])
    rre, rim = (right[..., :NF], right[..., NF:])
    return jnp.concatenate([lre * rre + lim * rim, lim * rre - lre * rim], axis=-1).astype(jnp.bfloat16)

def orthonormal(raw):
    highest = lax.Precision.HIGHEST
    gram = jnp.dot(raw, raw.T, precision=highest)
    lower = jnp.linalg.cholesky(gram)
    return lax.linalg.triangular_solve(lower, raw, left_side=True, lower=True)

def reference(records, pair_list, sketch):
    highest = lax.Precision.HIGHEST
    forward, inverse = tables()
    white = lax.map(lambda block: whiten(block, forward), records)

    def one_pair(pair):
        cross = correlate(white[pair[0]], white[pair[1]])
        lagged = jnp.dot(cross.astype(jnp.float32), inverse.astype(jnp.float32), preferred_element_type=jnp.float32)
        crossf = cross.astype(jnp.float32)
        energy = jnp.sum(crossf * crossf)
        probe = jnp.dot(lagged, sketch.T, precision=highest)
        raw = jnp.dot(probe.T, lagged, precision=highest)
        basis = orthonormal(raw)
        coeffs = jnp.dot(lagged, basis.T, precision=highest)
        total = lax.optimization_barrier(jnp.sum(coeffs, axis=0))
        power = lax.optimization_barrier(jnp.sum(coeffs * coeffs, axis=0))
        gain = power / (power + energy / (2 * NF))
        return jnp.dot(gain * total / WINDOWS, basis, precision=highest)
    return lax.map(one_pair, pair_list)
```

```python
import math

import jax
import jax.numpy as jnp
import numpy as np
from jax import lax
from jax.experimental import pallas as pl
from jax.experimental.pallas import tpu as pltpu
from jax.sharding import PartitionSpec as P

SAMPLES = 2048
NF = 512
LAGS = 2048
RANK = 16
CAP = 12
PAIRS_DEV = 128
F0 = NF // 2
STEP = 32
ISTEP = 16
F32 = jnp.float32
BF16 = jnp.bfloat16


def turns(first, second):
    k = np.mod(np.asarray(first)[:, None] * np.asarray(second)[None, :], SAMPLES)
    return k.astype(np.float64) * (2.0 * math.pi / SAMPLES)


def table_parts():
    freq = F0 + np.arange(NF)
    base = turns(np.arange(0, SAMPLES // 2, STEP), freq)
    step = turns(np.arange(STEP), freq)
    forward = (np.stack([np.cos(base), np.sin(base)]), np.stack([np.cos(step), np.sin(step)]))
    shifts = np.arange(LAGS) - LAGS // 2
    ibase = turns(F0 + np.arange(0, NF, ISTEP), shifts)
    istep = turns(np.arange(ISTEP), shifts)
    inverse = (
        np.stack([np.cos(ibase), np.sin(ibase)]) / math.sqrt(NF),
        np.stack([np.cos(istep), np.sin(istep)]),
    )
    return tuple(p.astype(np.float32) for p in forward + inverse)


def gram_excess():
    freq = F0 + np.arange(NF)
    shifts = np.arange(LAGS) - LAGS // 2
    angle = np.mod(freq[:, None] * shifts[None, :], SAMPLES).astype(np.float32)
    angle = angle * np.float32(2.0 * math.pi / SAMPLES)
    root = np.float32(math.sqrt(NF))
    blocks = []
    for wave in (np.cos(angle), -np.sin(angle)):
        rows = (wave / root).astype(jnp.bfloat16).astype(np.float64)
        blocks.append(rows @ rows.T - 2.0 * np.eye(NF))
    return np.stack(blocks).astype(np.float32).astype(jnp.bfloat16)


def split3(x):
    high = x.astype(BF16)
    rest = x - high.astype(F32)
    mid = rest.astype(BF16)
    low = (rest - mid.astype(F32)).astype(BF16)
    return jnp.concatenate([high, mid, low], axis=0)


def split2(x):
    high = x.astype(BF16)
    return jnp.concatenate([high, (x - high.astype(F32)).astype(BF16)], axis=0)


def sum3(x):
    n = x.shape[0] // 3
    return x[:n] + x[n : 2 * n] + x[2 * n :]


def dot_nt(a, b, precision=None):
    return lax.dot_general(
        a, b, (((1,), (1,)), ((), ())), preferred_element_type=F32, precision=precision
    )


def dot_nn(a, b):
    return jnp.dot(a, b, preferred_element_type=F32)


def whiten_kernel(sel_ref, rec_ref, base_ref, step_ref, out_ref, table, white):
    i = pl.program_id(0)

    @pl.when(i == 0)
    def _():
        parity = lax.broadcasted_iota(jnp.int32, (1, NF), 1) & 1
        sign = 1.0 - 2.0 * parity.astype(F32)
        cos_step = step_ref[0]
        sin_step = step_ref[1]

        def body(n, carry):
            cos_base = base_ref[0, pl.ds(n, 1), :]
            sin_base = base_ref[1, pl.ds(n, 1), :]
            cos = cos_base * cos_step - sin_base * sin_step
            sin = sin_base * cos_step + cos_base * sin_step
            row = pl.multiple_of(n * STEP, STEP)
            far = pl.multiple_of(n * STEP + SAMPLES // 2, STEP)
            table[pl.ds(row, STEP), :NF] = cos.astype(BF16)
            table[pl.ds(row, STEP), NF:] = sin.astype(BF16)
            table[pl.ds(far, STEP), :NF] = (cos * sign).astype(BF16)
            table[pl.ds(far, STEP), NF:] = (sin * sign).astype(BF16)
            return carry

        lax.fori_loop(0, SAMPLES // 2 // STEP, body, 0)

    spectra = dot_nn(rec_ref[...], table[...])
    re = spectra[:, :NF]
    im = spectra[:, NF:]
    power = re * re + im * im
    level = jnp.mean(power, axis=1, keepdims=True)
    factor = lax.rsqrt(power + level + 1e-06)
    rows = jnp.concatenate([re * factor, im * factor], axis=1).astype(BF16)
    channels, windows, width = white.shape
    per = rec_ref.shape[0] // windows
    white[pl.ds(i * per, per)] = rows.reshape(per, windows, width)

    @pl.when(i == pl.num_programs(0) - 1)
    def _():
        def body(n, carry):
            out_ref[n] = white[sel_ref[n]]
            return carry

        lax.fori_loop(0, out_ref.shape[0], body, 0)


def whiten(records, sel, base, step):
    ch_dev, win_dev, samples = records.shape
    rows = ch_dev * win_dev
    block = 256
    full = lambda i, sel: (0, 0, 0)
    return pl.pallas_call(
        whiten_kernel,
        out_shape=jax.ShapeDtypeStruct((sel.shape[0], win_dev, 2 * NF), BF16),
        grid_spec=pltpu.PrefetchScalarGridSpec(
            num_scalar_prefetch=1,
            grid=(rows // block,),
            in_specs=[
                pl.BlockSpec((block, samples), lambda i, sel: (i, 0)),
                pl.BlockSpec(base.shape, full),
                pl.BlockSpec(step.shape, full),
            ],
            out_specs=pl.BlockSpec((sel.shape[0], win_dev, 2 * NF), full),
            scratch_shapes=[
                pltpu.VMEM((samples, 2 * NF), BF16),
                pltpu.VMEM((ch_dev, win_dev, 2 * NF), BF16),
            ],
        ),
        compiler_params=pltpu.CompilerParams(
            dimension_semantics=("arbitrary",), vmem_limit_bytes=48 << 20
        ),
        name="whiten",
    )(sel, records.reshape(rows, samples), base, step)


def inverse_kernel(sketch_ref, base_ref, step_ref, inv_ref, s3_ref):
    cos_step = step_ref[0]
    sin_step = step_ref[1]

    def body(n, carry):
        cos_base = base_ref[0, pl.ds(n, 1), :]
        sin_base = base_ref[1, pl.ds(n, 1), :]
        cos = cos_base * cos_step - sin_base * sin_step
        sin = sin_base * cos_step + cos_base * sin_step
        row = pl.multiple_of(n * ISTEP, ISTEP)
        low = pl.multiple_of(n * ISTEP + NF, ISTEP)
        inv_ref[pl.ds(row, ISTEP), :] = cos.astype(BF16)
        inv_ref[pl.ds(low, ISTEP), :] = (-sin).astype(BF16)
        return carry

    lax.fori_loop(0, NF // ISTEP, body, 0)
    s3_ref[...] = split3(sum3(dot_nt(split3(sketch_ref[...]), inv_ref[...])))


def inverse_table(sketch, base, step):
    return pl.pallas_call(
        inverse_kernel,
        out_shape=(
            jax.ShapeDtypeStruct((2 * NF, LAGS), BF16),
            jax.ShapeDtypeStruct((3 * RANK, 2 * NF), BF16),
        ),
        compiler_params=pltpu.CompilerParams(vmem_limit_bytes=32 << 20),
        name="inverse_table",
    )(sketch, base, step)


def cross_kernel(slot_ref, arr_ref, out_ref):
    i = pl.program_id(0)
    group = out_ref.shape[1]
    for q in range(group):
        left = arr_ref[slot_ref[0, i * group + q]].astype(F32)
        right = arr_ref[slot_ref[1, i * group + q]].astype(F32)
        lre, lim = left[:, :NF], left[:, NF:]
        rre, rim = right[:, :NF], right[:, NF:]
        out_ref[0, q, :, :NF] = (lre * rre + lim * rim).astype(BF16)
        out_ref[0, q, :, NF:] = (lim * rre - lre * rim).astype(BF16)


def correlate(slots, arrived, parts):
    windows = arrived.shape[1]
    group = PAIRS_DEV // parts
    return pl.pallas_call(
        cross_kernel,
        out_shape=jax.ShapeDtypeStruct((parts, group, windows, 2 * NF), BF16),
        grid_spec=pltpu.PrefetchScalarGridSpec(
            num_scalar_prefetch=1,
            grid=(parts,),
            in_specs=[pl.BlockSpec(arrived.shape, lambda i, s: (0, 0, 0))],
            out_specs=pl.BlockSpec((1, group, windows, 2 * NF), lambda i, s: (i, 0, 0, 0)),
        ),
        compiler_params=pltpu.CompilerParams(
            dimension_semantics=("arbitrary",), vmem_limit_bytes=32 << 20
        ),
        name="cross",
    )(slots, arrived)


def stack_kernel(c_ref, s3_ref, e_ref, o_ref, r_s, h_s, y_s, g_s, en_s):
    parts, group, windows, width = c_ref.shape
    count = parts * windows
    s3 = s3_ref[...]
    probes = []
    for p in range(group):
        c = c_ref[:, p].reshape(count, width)
        probe = sum3(dot_nt(s3, c))
        probes.append(probe)
        r_s[:, p, :] = sum3(dot_nn(split3(probe), c))
        cf = c.astype(F32)
        en_s[pl.ds(p, 1), :] = jnp.sum(cf * cf, axis=0, keepdims=True)
    raw = r_s[...].reshape(RANK * group, width)
    raw2 = split2(raw)
    rows = RANK * group
    for half in range(2):
        lanes = slice(half * NF, (half + 1) * NF)
        more = dot_nn(raw2[:, lanes], e_ref[half])
        full = 2.0 * raw[:, lanes] + (more[:rows] + more[rows:])
        h_s[:, :, lanes] = full.reshape(RANK, group, NF)
    lane = lax.broadcasted_iota(jnp.int32, (RANK, 128), 1)
    row = lax.broadcasted_iota(jnp.int32, (RANK, 128), 0)
    unit = (lane == row + RANK).astype(F32)
    for p in range(group):
        c = c_ref[:, p].reshape(count, width)
        y = sum3(dot_nt(split3(h_s[:, p, :]), c))
        gram = dot_nt(y, probes[p], lax.Precision.HIGHEST)
        y_s[:, p, :] = y
        g_s[:, p, :] = unit
        g_s[:, p, :RANK] = gram
    ys = [y_s[r] for r in range(RANK)]
    gs = [g_s[r] for r in range(RANK)]
    for k in range(RANK):
        pivot = gs[k][:, k : k + 1]
        scale = lax.rsqrt(pivot)
        scale = scale * (1.5 - 0.5 * pivot * scale * scale)
        gs[k] = gs[k] * scale
        ys[k] = ys[k] * scale
        for r in range(k + 1, RANK):
            factor = gs[r][:, k : k + 1] * scale
            gs[r] = gs[r] - factor * gs[k]
            ys[r] = ys[r] - factor * ys[k]
    energy = jnp.sum(en_s[...], axis=1, keepdims=True)
    mix = jnp.zeros_like(gs[0])
    for r in range(RANK):
        power = jnp.sum(ys[r] * ys[r], axis=1, keepdims=True)
        total = jnp.sum(ys[r], axis=1, keepdims=True)
        gain = power / (power + energy / (2 * NF))
        mix = mix + (gain * total / count) * gs[r]
    stack = jnp.zeros((group, width), F32)
    for r in range(RANK):
        stack = stack + mix[:, RANK + r : RANK + r + 1] * r_s[r]
    for t in range(parts):
        o_ref[t] = stack


def stack_up(cross, s3, excess):
    parts, group, windows, width = cross.shape
    return pl.pallas_call(
        stack_kernel,
        out_shape=jax.ShapeDtypeStruct((parts, group, width), F32),
        scratch_shapes=[
            pltpu.VMEM((RANK, group, width), F32),
            pltpu.VMEM((RANK, group, width), F32),
            pltpu.VMEM((RANK, group, parts * windows), F32),
            pltpu.VMEM((RANK, group, 128), F32),
            pltpu.VMEM((group, width), F32),
        ],
        compiler_params=pltpu.CompilerParams(vmem_limit_bytes=48 << 20),
        name="stack",
    )(cross, s3, excess)


def lags_kernel(x_ref, inv_ref, o_ref, x2):
    rows = x_ref.shape[0]

    @pl.when(pl.program_id(0) == 0)
    def _():
        x2[...] = split2(x_ref[...])

    y = dot_nn(x2[...], inv_ref[...])
    o_ref[...] = y[:rows] + y[rows:]


def to_lags(x, inverse):
    rows, width = x.shape
    block = 512
    return pl.pallas_call(
        lags_kernel,
        out_shape=jax.ShapeDtypeStruct((rows, LAGS), F32),
        grid=(LAGS // block,),
        in_specs=[
            pl.BlockSpec((rows, width), lambda i: (0, 0)),
            pl.BlockSpec((width, block), lambda i: (0, i)),
        ],
        out_specs=pl.BlockSpec((rows, block), lambda i: (0, i)),
        scratch_shapes=[pltpu.VMEM((2 * rows, width), BF16)],
        compiler_params=pltpu.CompilerParams(
            dimension_semantics=("arbitrary",), vmem_limit_bytes=32 << 20
        ),
        name="lags",
    )(x, inverse)


def local(records, pair_list, sketch):
    base, step, ibase, istep = table_parts()
    n_pair = lax.axis_size("pair")
    n_tm = lax.axis_size("tm")
    owner = lax.axis_index("pair")
    ch_dev, win_dev, _ = records.shape

    wanted = pair_list.reshape(n_pair, 2 * PAIRS_DEV) - owner * ch_dev
    column = jnp.arange(ch_dev)
    asked = jnp.any(wanted[:, :, None] == column[None, None, :], axis=1)
    before = jnp.sum(asked[:, :, None] & (column[:, None] < column[None, :]), axis=1)
    slot = jnp.arange(CAP)
    picked = asked[:, None, :] & (before[:, None, :] == slot[None, :, None])
    sel = jnp.sum(jnp.where(picked, column, 0), axis=2).astype(jnp.int32).reshape(-1)
    outgoing = whiten(records, sel, base, step)

    mine = lax.dynamic_slice_in_dim(pair_list, owner * PAIRS_DEV, PAIRS_DEV, 0).T
    everyone = jnp.arange(n_pair * ch_dev)
    held = jnp.any(mine.reshape(-1)[:, None] == everyone[None, :], axis=0)
    block = mine // ch_dev
    first = (block * ch_dev)[:, :, None]
    ahead = held & (everyone >= first) & (everyone < mine[:, :, None])
    slots = (block * CAP + jnp.sum(ahead, axis=2)).astype(jnp.int32)

    arrived = lax.all_to_all(
        outgoing.reshape(n_pair, CAP, win_dev, 2 * NF), "pair", 0, 0, tiled=True
    ).reshape(n_pair * CAP, win_dev, 2 * NF)
    inverse, s3 = inverse_table(sketch, ibase, istep)
    cross = correlate(slots, arrived, n_tm)
    cross = lax.all_to_all(cross, "tm", 0, 0, tiled=True)
    stack = stack_up(cross, s3, gram_excess())
    stack = lax.all_to_all(stack, "tm", 0, 0, tiled=True)
    return to_lags(stack.reshape(PAIRS_DEV, 2 * NF), inverse)


def solution(mesh):
    in_specs = (P("pair", "tm", None), P(), P())
    out_specs = P("pair", None)
    return jax.shard_map(local, mesh=mesh, in_specs=in_specs, out_specs=out_specs, check_vma=False)
```

```python
import math

import jax
import jax.numpy as jnp
import numpy as np
from jax import lax
from jax.experimental import pallas as pl
from jax.experimental.pallas import tpu as pltpu
from jax.sharding import PartitionSpec as P

SAMPLES = 2048
NF = 512
LAGS = 2048
RANK = 16
CAP = 12
PAIRS_DEV = 128
F0 = NF // 2
STEP = 32
ISTEP = 16
CHUNKS = ((0, 256), (256, 512))
F32 = jnp.float32
BF16 = jnp.bfloat16


def turns(first, second):
    k = np.mod(np.asarray(first)[:, None] * np.asarray(second)[None, :], SAMPLES)
    return k.astype(np.float64) * (2.0 * math.pi / SAMPLES)


def table_parts():
    freq = F0 + np.arange(NF)
    base = turns(np.arange(0, SAMPLES // 2, STEP), freq)
    step = turns(np.arange(STEP), freq)
    forward = (np.stack([np.cos(base), np.sin(base)]), np.stack([np.cos(step), np.sin(step)]))
    shifts = np.arange(LAGS) - LAGS // 2
    ibase = turns(F0 + np.arange(0, NF, ISTEP), shifts)
    istep = turns(np.arange(ISTEP), shifts)
    inverse = (
        np.stack([np.cos(ibase), np.sin(ibase)]) / math.sqrt(NF),
        np.stack([np.cos(istep), np.sin(istep)]),
    )
    return tuple(p.astype(np.float32) for p in forward + inverse)


def gram_excess():
    freq = F0 + np.arange(NF)
    shifts = np.arange(LAGS) - LAGS // 2
    angle = np.mod(freq[:, None] * shifts[None, :], SAMPLES).astype(np.float32)
    angle = angle * np.float32(2.0 * math.pi / SAMPLES)
    root = np.float32(math.sqrt(NF))
    blocks = []
    for wave in (np.cos(angle), -np.sin(angle)):
        rows = (wave / root).astype(jnp.bfloat16).astype(np.float64)
        blocks.append(rows @ rows.T - 2.0 * np.eye(NF))
    return np.stack(blocks).astype(np.float32).astype(jnp.bfloat16)


def in_hbm(x):
    return pltpu.with_memory_space_constraint(x, pltpu.HBM)


def split3(x):
    high = x.astype(BF16)
    rest = x - high.astype(F32)
    mid = rest.astype(BF16)
    low = (rest - mid.astype(F32)).astype(BF16)
    return jnp.concatenate([high, mid, low], axis=0)


def split2(x):
    high = x.astype(BF16)
    return jnp.concatenate([high, (x - high.astype(F32)).astype(BF16)], axis=0)


def sum3(x):
    n = x.shape[0] // 3
    return x[:n] + x[n : 2 * n] + x[2 * n :]


def dot_nt(a, b, precision=None):
    return lax.dot_general(
        a, b, (((1,), (1,)), ((), ())), preferred_element_type=F32, precision=precision
    )


def dot_nn(a, b):
    return jnp.dot(a, b, preferred_element_type=F32)


def cut(rows, lo, hi):
    return jnp.concatenate([rows[:, lo:hi], rows[:, NF + lo : NF + hi]], axis=1)


def pick(pair_ref, owner, channels, peers):
    shape = (channels, PAIRS_DEV)
    column = lax.broadcasted_iota(jnp.int32, shape, 0)
    lane = lax.broadcasted_iota(jnp.int32, shape, 1)
    asked = jnp.zeros(shape, F32)
    for d in range(peers):
        named = pair_ref[:, d * PAIRS_DEV : (d + 1) * PAIRS_DEV] - owner * channels
        hit = (column == named[0:1]) | (column == named[1:2])
        seen = jnp.max(hit.astype(F32), axis=1, keepdims=True)
        asked = jnp.where(lane == d, seen, asked)
    square = (channels, channels)
    earlier = lax.broadcasted_iota(jnp.int32, square, 1) < lax.broadcasted_iota(jnp.int32, square, 0)
    before = dot_nn(earlier.astype(F32).astype(BF16), asked.astype(BF16))
    number = column.astype(F32) * asked
    rows = []
    for k in range(CAP):
        rows.append(jnp.sum(jnp.where(before == k, number, 0.0), axis=0, keepdims=True))
    return jnp.concatenate(rows, axis=0).astype(jnp.int32)


def whiten_kernel(owner_ref, pair_ref, rec_ref, parts_ref, *rest):
    count = 1 + (len(CHUNKS) - 1) * (pair_ref.shape[1] // PAIRS_DEV)
    outs, bufs, rest = rest[:count], rest[count : 2 * count], rest[2 * count :]
    table, white, chosen, sel_ref, chosen_sem, sems = rest
    i = pl.program_id(0)
    peers = pair_ref.shape[1] // PAIRS_DEV
    owner = owner_ref[0]
    fetch = pltpu.make_async_copy(chosen, sel_ref, chosen_sem)

    @pl.when(i == 0)
    def _():
        chosen[...] = pick(pair_ref, owner, white.shape[0], peers)
        fetch.start()
        parity = lax.broadcasted_iota(jnp.int32, (1, NF), 1) & 1
        sign = 1.0 - 2.0 * parity.astype(F32)
        cos_step = parts_ref[2]
        sin_step = parts_ref[3]

        def body(n, carry):
            cos_base = parts_ref[0, pl.ds(n, 1), :]
            sin_base = parts_ref[1, pl.ds(n, 1), :]
            cos = cos_base * cos_step - sin_base * sin_step
            sin = sin_base * cos_step + cos_base * sin_step
            row = pl.multiple_of(n * STEP, STEP)
            far = pl.multiple_of(n * STEP + SAMPLES // 2, STEP)
            table[pl.ds(row, STEP), :NF] = cos.astype(BF16)
            table[pl.ds(row, STEP), NF:] = sin.astype(BF16)
            table[pl.ds(far, STEP), :NF] = (cos * sign).astype(BF16)
            table[pl.ds(far, STEP), NF:] = (sin * sign).astype(BF16)
            return carry

        lax.fori_loop(0, SAMPLES // 2 // STEP, body, 0)

    spectra = dot_nn(rec_ref[...], table[...])
    re = spectra[:, :NF]
    im = spectra[:, NF:]
    power = re * re + im * im
    level = jnp.mean(power, axis=1, keepdims=True)
    factor = lax.rsqrt(power + level + 1e-06)
    rows = jnp.concatenate([re * factor, im * factor], axis=1).astype(BF16)
    channels, windows, width = white.shape
    per = rec_ref.shape[0] // windows
    white[pl.ds(i * per, per)] = rows.reshape(per, windows, width)

    @pl.when(i == pl.num_programs(0) - 1)
    def _():
        fetch.wait()
        sends = []

        def fill(buf, row, peer, lo, hi):
            def body(n, carry):
                buf[row + n] = cut(white[sel_ref[n, peer]], lo, hi)
                return carry

            lax.fori_loop(0, CAP, body, 0, unroll=4)

        for d in range(peers):
            fill(bufs[0], d * CAP, d, *CHUNKS[0])
        sends.append(pltpu.make_async_copy(bufs[0], outs[0], sems.at[0]))
        sends[-1].start()
        for j, (lo, hi) in enumerate(CHUNKS[1:]):
            for x in range(peers):
                n = 1 + j * peers + x
                fill(bufs[n], 0, owner ^ x, lo, hi)
                sends.append(pltpu.make_async_copy(bufs[n], outs[n], sems.at[n]))
                sends[-1].start()
        for send in sends:
            send.wait()


def whiten(records, pairs, owner, parts):
    ch_dev, win_dev, samples = records.shape
    rows = ch_dev * win_dev
    block = 256
    peers = pairs.shape[1] // PAIRS_DEV
    shapes = [(peers * CAP, win_dev, 2 * (CHUNKS[0][1] - CHUNKS[0][0]))]
    for lo, hi in CHUNKS[1:]:
        shapes += [(CAP, win_dev, 2 * (hi - lo))] * peers
    outs = pl.pallas_call(
        whiten_kernel,
        out_shape=[pltpu.HBM(shape, BF16) for shape in shapes],
        grid_spec=pltpu.PrefetchScalarGridSpec(
            num_scalar_prefetch=1,
            grid=(rows // block,),
            in_specs=[
                pl.BlockSpec(pairs.shape, lambda i, owner: (0, 0)),
                pl.BlockSpec((block, samples), lambda i, owner: (i, 0)),
                pl.BlockSpec(parts.shape, lambda i, owner: (0, 0, 0)),
            ],
            out_specs=[pl.BlockSpec(memory_space=pltpu.HBM)] * len(shapes),
            scratch_shapes=[pltpu.VMEM(shape, BF16) for shape in shapes]
            + [
                pltpu.VMEM((samples, 2 * NF), BF16),
                pltpu.VMEM((ch_dev, win_dev, 2 * NF), BF16),
                pltpu.VMEM((CAP, PAIRS_DEV), jnp.int32),
                pltpu.SMEM((CAP, PAIRS_DEV), jnp.int32),
                pltpu.SemaphoreType.DMA,
                pltpu.SemaphoreType.DMA((len(shapes),)),
            ],
        ),
        compiler_params=pltpu.CompilerParams(
            dimension_semantics=("arbitrary",), vmem_limit_bytes=24 << 20
        ),
        name="whiten",
    )(owner, *map(in_hbm, (pairs, records.reshape(rows, samples), parts)))
    return outs[0], [outs[1 + j * peers : 1 + (j + 1) * peers] for j in range(len(CHUNKS) - 1)]


def inverse_kernel(sketch_ref, base_ref, step_ref, inv_ref, s3_ref):
    cos_step = step_ref[0]
    sin_step = step_ref[1]

    def body(n, carry):
        cos_base = base_ref[0, pl.ds(n, 1), :]
        sin_base = base_ref[1, pl.ds(n, 1), :]
        cos = cos_base * cos_step - sin_base * sin_step
        sin = sin_base * cos_step + cos_base * sin_step
        row = pl.multiple_of(n * ISTEP, ISTEP)
        low = pl.multiple_of(n * ISTEP + NF, ISTEP)
        inv_ref[pl.ds(row, ISTEP), :] = cos.astype(BF16)
        inv_ref[pl.ds(low, ISTEP), :] = (-sin).astype(BF16)
        return carry

    lax.fori_loop(0, NF // ISTEP, body, 0)
    s3_ref[...] = split3(sum3(dot_nt(split3(sketch_ref[...]), inv_ref[...])))


def inverse_table(sketch, base, step):
    return pl.pallas_call(
        inverse_kernel,
        out_shape=(
            jax.ShapeDtypeStruct((2 * NF, LAGS), BF16),
            jax.ShapeDtypeStruct((3 * RANK, 2 * NF), BF16),
        ),
        compiler_params=pltpu.CompilerParams(vmem_limit_bytes=12 << 20),
        name="inverse_table",
    )(sketch, base, step)


def cross_kernel(slot_ref, *rest):
    if len(rest) == 2:
        arr, out_ref = rest
    else:
        blocks, (out_ref, arr) = rest[:-2], rest[-2:]

        @pl.when(pl.program_id(0) == 0)
        def _():
            size = blocks[0].shape[0]
            for n, block in enumerate(blocks):
                arr[n * size : (n + 1) * size] = block[...]

    i = pl.program_id(0)
    some, group = out_ref.shape[:2]
    bins = out_ref.shape[3] // 2

    def body(n, carry):
        at = (i * some + n) * group
        for q in range(group):
            left = arr[slot_ref[0, at + q]].astype(F32)
            right = arr[slot_ref[1, at + q]].astype(F32)
            lre, lim = left[:, :bins], left[:, bins:]
            rre, rim = right[:, :bins], right[:, bins:]
            out_ref[n, q, :, :bins] = (lre * rre + lim * rim).astype(BF16)
            out_ref[n, q, :, bins:] = (lim * rre - lre * rim).astype(BF16)
        return carry

    lax.fori_loop(0, some, body, 0)


def correlate(slots, blocks, parts):
    size, windows, width = blocks[0].shape
    group = PAIRS_DEV // parts
    some = 4 if parts % 4 == 0 else 1
    scratch = []
    if len(blocks) > 1:
        scratch = [pltpu.VMEM((size * len(blocks), windows, width), BF16)]
    return pl.pallas_call(
        cross_kernel,
        out_shape=jax.ShapeDtypeStruct((parts, group, windows, width), BF16),
        grid_spec=pltpu.PrefetchScalarGridSpec(
            num_scalar_prefetch=1,
            grid=(parts // some,),
            in_specs=[pl.BlockSpec(blocks[0].shape, lambda i, s: (0, 0, 0))] * len(blocks),
            out_specs=pl.BlockSpec((some, group, windows, width), lambda i, s: (i, 0, 0, 0)),
            scratch_shapes=scratch,
        ),
        compiler_params=pltpu.CompilerParams(
            dimension_semantics=("arbitrary",), vmem_limit_bytes=12 << 20
        ),
        name="cross",
    )(slots, *blocks)


def stack_kernel(*refs):
    c_refs, refs = refs[: len(CHUNKS)], refs[len(CHUNKS) :]
    s3_ref, e_ref, o_ref, r_s, h_s, y_s, g_s, en_s = refs
    parts, group, windows, _ = c_refs[0].shape
    width = 2 * NF
    count = parts * windows
    s3 = s3_ref[...]

    def pair(p):
        pieces = [c_ref[:, p].reshape(count, c_ref.shape[3]) for c_ref in c_refs]
        halves = [piece.shape[1] // 2 for piece in pieces]
        real = [piece[:, :n] for piece, n in zip(pieces, halves)]
        imag = [piece[:, n:] for piece, n in zip(pieces, halves)]
        return jnp.concatenate(real + imag, axis=1)

    probes = []
    for p in range(group):
        c = pair(p)
        probe = sum3(dot_nt(s3, c))
        probes.append(probe)
        r_s[:, p, :] = sum3(dot_nn(split3(probe), c))
        cf = c.astype(F32)
        en_s[pl.ds(p, 1), :] = jnp.sum(cf * cf, axis=0, keepdims=True)
    raw = r_s[...].reshape(RANK * group, width)
    raw2 = split2(raw)
    rows = RANK * group
    for half in range(2):
        lanes = slice(half * NF, (half + 1) * NF)
        more = dot_nn(raw2[:, lanes], e_ref[half])
        full = 2.0 * raw[:, lanes] + (more[:rows] + more[rows:])
        h_s[:, :, lanes] = full.reshape(RANK, group, NF)
    lane = lax.broadcasted_iota(jnp.int32, (RANK, 128), 1)
    row = lax.broadcasted_iota(jnp.int32, (RANK, 128), 0)
    unit = (lane == row + RANK).astype(F32)
    for p in range(group):
        c = pair(p)
        y = sum3(dot_nt(split3(h_s[:, p, :]), c))
        gram = dot_nt(y, probes[p], lax.Precision.HIGHEST)
        y_s[:, p, :] = y
        g_s[:, p, :] = unit
        g_s[:, p, :RANK] = gram
    ys = [y_s[r] for r in range(RANK)]
    gs = [g_s[r] for r in range(RANK)]
    for k in range(RANK):
        pivot = gs[k][:, k : k + 1]
        scale = lax.rsqrt(pivot)
        scale = scale * (1.5 - 0.5 * pivot * scale * scale)
        gs[k] = gs[k] * scale
        ys[k] = ys[k] * scale
        for r in range(k + 1, RANK):
            factor = gs[r][:, k : k + 1] * scale
            gs[r] = gs[r] - factor * gs[k]
            ys[r] = ys[r] - factor * ys[k]
    energy = jnp.sum(en_s[...], axis=1, keepdims=True)
    mix = jnp.zeros_like(gs[0])
    for r in range(RANK):
        power = jnp.sum(ys[r] * ys[r], axis=1, keepdims=True)
        total = jnp.sum(ys[r], axis=1, keepdims=True)
        gain = power / (power + energy / (2 * NF))
        mix = mix + (gain * total / count) * gs[r]
    stack = jnp.zeros((group, width), F32)
    for r in range(RANK):
        stack = stack + mix[:, RANK + r : RANK + r + 1] * r_s[r]
    for t in range(parts):
        o_ref[t] = stack


def stack_up(crosses, s3, excess):
    parts, group, windows, _ = crosses[0].shape
    width = 2 * NF
    return pl.pallas_call(
        stack_kernel,
        out_shape=jax.ShapeDtypeStruct((parts, group, width), F32),
        scratch_shapes=[
            pltpu.VMEM((RANK, group, width), F32),
            pltpu.VMEM((RANK, group, width), F32),
            pltpu.VMEM((RANK, group, parts * windows), F32),
            pltpu.VMEM((RANK, group, 128), F32),
            pltpu.VMEM((group, width), F32),
        ],
        compiler_params=pltpu.CompilerParams(vmem_limit_bytes=24 << 20),
        name="stack",
    )(*crosses, s3, excess)


def lags_kernel(x_ref, inv_ref, o_ref, x2):
    rows = x_ref.shape[0]

    @pl.when(pl.program_id(0) == 0)
    def _():
        x2[...] = split2(x_ref[...])

    y = dot_nn(x2[...], inv_ref[...])
    o_ref[...] = y[:rows] + y[rows:]


def to_lags(x, inverse):
    rows, width = x.shape
    block = 512
    return pl.pallas_call(
        lags_kernel,
        out_shape=jax.ShapeDtypeStruct((rows, LAGS), F32),
        grid=(LAGS // block,),
        in_specs=[
            pl.BlockSpec((rows, width), lambda i: (0, 0)),
            pl.BlockSpec((width, block), lambda i: (0, i)),
        ],
        out_specs=pl.BlockSpec((rows, block), lambda i: (0, i)),
        scratch_shapes=[pltpu.VMEM((2 * rows, width), BF16)],
        compiler_params=pltpu.CompilerParams(
            dimension_semantics=("arbitrary",), vmem_limit_bytes=12 << 20
        ),
        name="lags",
    )(x, inverse)


def local(records, pair_list, sketch):
    base, step, ibase, istep = table_parts()
    n_pair = lax.axis_size("pair")
    n_tm = lax.axis_size("tm")
    owner = lax.axis_index("pair")
    ch_dev, win_dev, _ = records.shape

    pairs = pair_list.T
    parts = np.concatenate([base, step])
    out_first, out_rest = whiten(records, pairs, owner.astype(jnp.int32).reshape(1), parts)

    mine = lax.dynamic_slice_in_dim(pairs, owner * PAIRS_DEV, PAIRS_DEV, 1)
    everyone = jnp.arange(n_pair * ch_dev)
    held = jnp.any(mine.reshape(-1)[:, None] == everyone[None, :], axis=0)
    block = mine // ch_dev
    first = (block * ch_dev)[:, :, None]
    ahead = held & (everyone >= first) & (everyone < mine[:, :, None])
    rank = jnp.sum(ahead, axis=2)
    slots = (block * CAP + rank).astype(jnp.int32)
    slots_rest = ((block ^ owner) * CAP + rank).astype(jnp.int32)

    shape = (n_pair, CAP) + out_first.shape[1:]
    arrived = lax.all_to_all(out_first.reshape(shape), "pair", 0, 0, tiled=True)
    inverse, s3 = inverse_table(sketch, ibase, istep)
    blocks = [arrived.reshape(out_first.shape)]
    blocks, out_rest, inverse, s3 = lax.optimization_barrier((blocks, out_rest, inverse, s3))
    crosses = []
    for j in range(len(CHUNKS)):
        cross = correlate(slots_rest if j else slots, blocks, n_tm)
        crosses.append(lax.all_to_all(cross, "tm", 0, 0, tiled=True))
        if j + 1 < len(CHUNKS):
            sent = out_rest[j]
            if j:
                blocks, sent = lax.optimization_barrier((blocks, sent))
            blocks = [sent[0]] + [
                lax.ppermute(sent[x], "pair", [(o, o ^ x) for o in range(n_pair)])
                for x in range(1, n_pair)
            ]
    stack = stack_up(crosses, s3, gram_excess())
    stack = lax.all_to_all(stack, "tm", 0, 0, tiled=True)
    return to_lags(stack.reshape(PAIRS_DEV, 2 * NF), inverse)


def solution(mesh):
    in_specs = (P("pair", "tm", None), P(), P())
    out_specs = P("pair", None)
    return jax.shard_map(local, mesh=mesh, in_specs=in_specs, out_specs=out_specs, check_vma=False)
```

```python
import functools
import math

import jax
import jax.numpy as jnp
import numpy as np
from jax import lax
from jax.experimental import pallas as pl
from jax.experimental.pallas import tpu as pltpu
from jax.sharding import PartitionSpec as P

SAMPLES = 2048
NF = 512
LAGS = 2048
RANK = 16
CAP = 12
PAIRS_DEV = 128
F0 = NF // 2
STEP = 32
ISTEP = 16
HALF = 8
F32 = jnp.float32
BF16 = jnp.bfloat16


def turns(first, second):
    k = np.mod(np.asarray(first)[:, None] * np.asarray(second)[None, :], SAMPLES)
    return k.astype(np.float64) * (2.0 * math.pi / SAMPLES)


def table_parts():
    freq = F0 + np.arange(NF)
    base = turns(np.arange(0, SAMPLES // 2, STEP), freq)
    step = turns(np.arange(STEP), freq)
    forward = (np.stack([np.cos(base), np.sin(base)]), np.stack([np.cos(step), np.sin(step)]))
    shifts = np.arange(LAGS) - LAGS // 2
    ibase = turns(F0 + np.arange(0, NF, ISTEP), shifts)
    istep = turns(np.arange(ISTEP), shifts)
    inverse = (
        np.stack([np.cos(ibase), np.sin(ibase)]) / math.sqrt(NF),
        np.stack([np.cos(istep), np.sin(istep)]),
    )
    return tuple(p.astype(np.float32) for p in forward + inverse)


def gram_excess():
    freq = F0 + np.arange(NF)
    shifts = np.arange(LAGS) - LAGS // 2
    angle = np.mod(freq[:, None] * shifts[None, :], SAMPLES).astype(np.float32)
    angle = angle * np.float32(2.0 * math.pi / SAMPLES)
    root = np.float32(math.sqrt(NF))
    blocks = []
    for wave in (np.cos(angle), -np.sin(angle)):
        rows = (wave / root).astype(jnp.bfloat16).astype(np.float64)
        blocks.append(rows @ rows.T - 2.0 * np.eye(NF))
    return np.stack(blocks).astype(np.float32).astype(jnp.bfloat16)


def in_hbm(x):
    return pltpu.with_memory_space_constraint(x, pltpu.HBM)


def split3(x):
    high = x.astype(BF16)
    rest = x - high.astype(F32)
    mid = rest.astype(BF16)
    low = (rest - mid.astype(F32)).astype(BF16)
    return jnp.concatenate([high, mid, low], axis=0)


def split2(x):
    high = x.astype(BF16)
    return jnp.concatenate([high, (x - high.astype(F32)).astype(BF16)], axis=0)


def sum3(x):
    n = x.shape[0] // 3
    return x[:n] + x[n : 2 * n] + x[2 * n :]


def dot_nt(a, b, precision=None):
    return lax.dot_general(
        a, b, (((1,), (1,)), ((), ())), preferred_element_type=F32, precision=precision
    )


def dot_nn(a, b):
    return jnp.dot(a, b, preferred_element_type=F32)


def pick(pair_ref, owner, channels, peers):
    shape = (channels, PAIRS_DEV)
    column = lax.broadcasted_iota(jnp.int32, shape, 0)
    lane = lax.broadcasted_iota(jnp.int32, shape, 1)
    asked = jnp.zeros(shape, F32)
    for d in range(peers):
        named = pair_ref[:, d * PAIRS_DEV : (d + 1) * PAIRS_DEV] - owner * channels
        hit = (column == named[0:1]) | (column == named[1:2])
        seen = jnp.max(hit.astype(F32), axis=1, keepdims=True)
        asked = jnp.where(lane == d, seen, asked)
    square = (channels, channels)
    earlier = lax.broadcasted_iota(jnp.int32, square, 1) < lax.broadcasted_iota(jnp.int32, square, 0)
    before = dot_nn(earlier.astype(F32).astype(BF16), asked.astype(BF16))
    number = column.astype(F32) * asked
    rows = []
    for k in range(CAP):
        rows.append(jnp.sum(jnp.where(before == k, number, 0.0), axis=0, keepdims=True))
    return jnp.concatenate(rows, axis=0).astype(jnp.int32)


def whiten_kernel(owner_ref, pair_ref, rec_ref, parts_ref, *rest, swapped):
    peers = pair_ref.shape[1] // PAIRS_DEV
    count = peers if swapped else 1
    outs, bufs, rest = rest[:count], rest[count : 2 * count], rest[2 * count :]
    table, white, chosen, sel_ref, chosen_sem, sems = rest
    i = pl.program_id(0)
    owner = owner_ref[0]
    fetch = pltpu.make_async_copy(chosen, sel_ref, chosen_sem)

    @pl.when(i == 0)
    def _():
        chosen[...] = pick(pair_ref, owner, white.shape[0], peers)
        fetch.start()
        parity = lax.broadcasted_iota(jnp.int32, (1, NF), 1) & 1
        sign = 1.0 - 2.0 * parity.astype(F32)
        cos_step = parts_ref[2]
        sin_step = parts_ref[3]

        def body(n, carry):
            cos_base = parts_ref[0, pl.ds(n, 1), :]
            sin_base = parts_ref[1, pl.ds(n, 1), :]
            cos = cos_base * cos_step - sin_base * sin_step
            sin = sin_base * cos_step + cos_base * sin_step
            row = pl.multiple_of(n * STEP, STEP)
            far = pl.multiple_of(n * STEP + SAMPLES // 2, STEP)
            table[pl.ds(row, STEP), :NF] = cos.astype(BF16)
            table[pl.ds(row, STEP), NF:] = sin.astype(BF16)
            table[pl.ds(far, STEP), :NF] = (cos * sign).astype(BF16)
            table[pl.ds(far, STEP), NF:] = (sin * sign).astype(BF16)
            return carry

        lax.fori_loop(0, SAMPLES // 2 // STEP, body, 0)

    per, windows, samples = rec_ref.shape
    spectra = dot_nn(rec_ref[...].reshape(per * windows, samples), table[...])
    re = spectra[:, :NF]
    im = spectra[:, NF:]
    power = re * re + im * im
    level = jnp.mean(power, axis=1, keepdims=True)
    factor = lax.rsqrt(power + level + 1e-06)
    rows = jnp.concatenate([re * factor, im * factor], axis=1).astype(BF16)
    white[pl.ds(i * per, per)] = rows.reshape(per, windows, 2 * NF)

    @pl.when(i == pl.num_programs(0) - 1)
    def _():
        fetch.wait()
        sends = []
        for d in range(peers):
            buf, first = (bufs[d], 0) if swapped else (bufs[0], d * CAP)
            peer = owner ^ d if swapped else d

            def body(n, carry, buf=buf, first=first, peer=peer):
                buf[first + n] = white[sel_ref[n, peer]]
                return carry

            lax.fori_loop(0, CAP, body, 0, unroll=4)
            if swapped:
                sends.append(pltpu.make_async_copy(buf, outs[d], sems.at[d]))
            else:
                span = pl.ds(first, CAP)
                sends.append(pltpu.make_async_copy(buf.at[span], outs[0].at[span], sems.at[d]))
            sends[-1].start()
        for send in sends:
            send.wait()


def whiten(records, pairs, owner, parts, half):
    ch_dev, _, samples = records.shape
    block = 32
    peers = pairs.shape[1] // PAIRS_DEV
    if half:
        shapes = [(CAP, HALF, 2 * NF)] * peers
    else:
        shapes = [(peers * CAP, HALF, 2 * NF)]
    return pl.pallas_call(
        functools.partial(whiten_kernel, swapped=bool(half)),
        out_shape=[pltpu.HBM(shape, BF16) for shape in shapes],
        grid_spec=pltpu.PrefetchScalarGridSpec(
            num_scalar_prefetch=1,
            grid=(ch_dev // block,),
            in_specs=[
                pl.BlockSpec(pairs.shape, lambda i, owner: (0, 0)),
                pl.BlockSpec((block, HALF, samples), lambda i, owner: (i, half, 0)),
                pl.BlockSpec(parts.shape, lambda i, owner: (0, 0, 0)),
            ],
            out_specs=[pl.BlockSpec(memory_space=pltpu.HBM)] * len(shapes),
            scratch_shapes=[pltpu.VMEM(shape, BF16) for shape in shapes]
            + [
                pltpu.VMEM((samples, 2 * NF), BF16),
                pltpu.VMEM((ch_dev, HALF, 2 * NF), BF16),
                pltpu.VMEM((CAP, PAIRS_DEV), jnp.int32),
                pltpu.SMEM((CAP, PAIRS_DEV), jnp.int32),
                pltpu.SemaphoreType.DMA,
                pltpu.SemaphoreType.DMA((peers,)),
            ],
        ),
        compiler_params=pltpu.CompilerParams(
            dimension_semantics=("arbitrary",), vmem_limit_bytes=24 << 20
        ),
        name="whiten",
    )(owner, *map(in_hbm, (pairs, records, parts)))


def inverse_kernel(sketch_ref, base_ref, step_ref, inv_ref, s3_ref):
    cos_step = step_ref[0]
    sin_step = step_ref[1]

    def body(n, carry):
        cos_base = base_ref[0, pl.ds(n, 1), :]
        sin_base = base_ref[1, pl.ds(n, 1), :]
        cos = cos_base * cos_step - sin_base * sin_step
        sin = sin_base * cos_step + cos_base * sin_step
        row = pl.multiple_of(n * ISTEP, ISTEP)
        low = pl.multiple_of(n * ISTEP + NF, ISTEP)
        inv_ref[pl.ds(row, ISTEP), :] = cos.astype(BF16)
        inv_ref[pl.ds(low, ISTEP), :] = (-sin).astype(BF16)
        return carry

    lax.fori_loop(0, NF // ISTEP, body, 0)
    s3_ref[...] = split3(sum3(dot_nt(split3(sketch_ref[...]), inv_ref[...]))).astype(F32).T.astype(BF16)


def inverse_table(sketch, base, step):
    return pl.pallas_call(
        inverse_kernel,
        out_shape=(
            jax.ShapeDtypeStruct((2 * NF, LAGS), BF16),
            jax.ShapeDtypeStruct((2 * NF, 3 * RANK), BF16),
        ),
        compiler_params=pltpu.CompilerParams(vmem_limit_bytes=12 << 20),
        name="inverse_table",
    )(sketch, base, step)


def cross_kernel(slot_ref, *rest):
    if len(rest) == 2:
        arr, out_ref = rest
    else:
        blocks, (out_ref, arr) = rest[:-2], rest[-2:]

        @pl.when(pl.program_id(0) == 0)
        def _():
            size = blocks[0].shape[0]
            for n, block in enumerate(blocks):
                arr[n * size : (n + 1) * size] = block[...]

    i = pl.program_id(0)
    some, group = out_ref.shape[:2]
    bins = out_ref.shape[3] // 2

    def body(n, carry):
        at = (i * some + n) * group
        for q in range(group):
            left = arr[slot_ref[0, at + q]].astype(F32)
            right = arr[slot_ref[1, at + q]].astype(F32)
            lre, lim = left[:, :bins], left[:, bins:]
            rre, rim = right[:, :bins], right[:, bins:]
            out_ref[n, q, :, :bins] = (lre * rre + lim * rim).astype(BF16)
            out_ref[n, q, :, bins:] = (lim * rre - lre * rim).astype(BF16)
        return carry

    lax.fori_loop(0, some, body, 0)


def correlate(slots, blocks, parts, space):
    size, windows, width = blocks[0].shape
    group = PAIRS_DEV // parts
    some = 4 if parts % 4 == 0 else 1
    scratch = []
    if len(blocks) > 1:
        scratch = [pltpu.VMEM((size * len(blocks), windows, width), BF16)]
    return pl.pallas_call(
        cross_kernel,
        out_shape=space((parts, group, windows, width), BF16),
        grid_spec=pltpu.PrefetchScalarGridSpec(
            num_scalar_prefetch=1,
            grid=(parts // some,),
            in_specs=[pl.BlockSpec(blocks[0].shape, lambda i, s: (0, 0, 0))] * len(blocks),
            out_specs=pl.BlockSpec((some, group, windows, width), lambda i, s: (i, 0, 0, 0)),
            scratch_shapes=scratch,
        ),
        compiler_params=pltpu.CompilerParams(
            dimension_semantics=("arbitrary",), vmem_limit_bytes=12 << 20
        ),
        name="cross",
    )(slots, *blocks)


def gather_pair(c_ref, p):
    parts, _, windows, width = c_ref.shape
    return c_ref[:, p].reshape(parts * windows, width)


def stack_kernel(ca_ref, cb_ref, s3_ref, e_ref, o_ref, r_s, h_s, y_s, g_s, en_s):
    parts, group, windows, width = ca_ref.shape
    count = 2 * parts * windows
    s3 = s3_ref[...]
    probes = []
    for p in range(group):
        c = jnp.concatenate([gather_pair(ca_ref, p), gather_pair(cb_ref, p)], axis=0)
        probe = sum3(dot_nn(c, s3).T)
        probes.append(probe)
        r_s[:, p, :] = sum3(dot_nn(split3(probe), c))
        cf = c.astype(F32)
        en_s[pl.ds(p, 1), :] = jnp.sum(cf * cf, axis=0, keepdims=True)
    raw = r_s[...].reshape(RANK * group, width)
    raw2 = split2(raw)
    rows = RANK * group
    for half in range(2):
        lanes = slice(half * NF, (half + 1) * NF)
        more = dot_nn(raw2[:, lanes], e_ref[half])
        full = 2.0 * raw[:, lanes] + (more[:rows] + more[rows:])
        h_s[:, :, lanes] = full.reshape(RANK, group, NF)
    lane = lax.broadcasted_iota(jnp.int32, (RANK, 128), 1)
    row = lax.broadcasted_iota(jnp.int32, (RANK, 128), 0)
    unit = (lane == row + RANK).astype(F32)
    for p in range(group):
        c = jnp.concatenate([gather_pair(ca_ref, p), gather_pair(cb_ref, p)], axis=0)
        y = sum3(dot_nt(split3(h_s[:, p, :]), c))
        gram = dot_nt(y, probes[p], lax.Precision.HIGHEST)
        y_s[:, p, :] = y
        g_s[:, p, :] = unit
        g_s[:, p, :RANK] = gram
    ys = [y_s[r] for r in range(RANK)]
    gs = [g_s[r] for r in range(RANK)]
    for k in range(RANK):
        pivot = gs[k][:, k : k + 1]
        scale = lax.rsqrt(pivot)
        scale = scale * (1.5 - 0.5 * pivot * scale * scale)
        gs[k] = gs[k] * scale
        ys[k] = ys[k] * scale
        for r in range(k + 1, RANK):
            factor = gs[r][:, k : k + 1] * scale
            gs[r] = gs[r] - factor * gs[k]
            ys[r] = ys[r] - factor * ys[k]
    energy = jnp.sum(en_s[...], axis=1, keepdims=True)
    mix = jnp.zeros_like(gs[0])
    for r in range(RANK):
        power = jnp.sum(ys[r] * ys[r], axis=1, keepdims=True)
        total = jnp.sum(ys[r], axis=1, keepdims=True)
        gain = power / (power + energy / (2 * NF))
        mix = mix + (gain * total / count) * gs[r]
    stack = jnp.zeros((group, width), F32)
    for r in range(RANK):
        stack = stack + mix[:, RANK + r : RANK + r + 1] * r_s[r]
    for t in range(parts):
        o_ref[t] = stack


def stack_up(crosses, s3, excess):
    parts, group, windows, width = crosses[0].shape
    return pl.pallas_call(
        stack_kernel,
        out_shape=jax.ShapeDtypeStruct((parts, group, width), F32),
        scratch_shapes=[
            pltpu.VMEM((RANK, group, width), F32),
            pltpu.VMEM((RANK, group, width), F32),
            pltpu.VMEM((RANK, group, 2 * parts * windows), F32),
            pltpu.VMEM((RANK, group, 128), F32),
            pltpu.VMEM((group, width), F32),
        ],
        compiler_params=pltpu.CompilerParams(vmem_limit_bytes=24 << 20),
        name="stack",
    )(*crosses, s3, excess)


def lags_kernel(x_ref, inv_ref, o_ref, x2):
    rows, block = o_ref.shape
    i = pl.program_id(0)

    @pl.when(i == 0)
    def _():
        x2[...] = split2(x_ref[...])

    y = dot_nn(x2[...], inv_ref[:, pl.ds(pl.multiple_of(i * block, block), block)])
    o_ref[...] = y[:rows] + y[rows:]


def to_lags(x, inverse):
    rows, width = x.shape
    block = 512
    return pl.pallas_call(
        lags_kernel,
        out_shape=jax.ShapeDtypeStruct((rows, LAGS), F32),
        grid=(LAGS // block,),
        in_specs=[
            pl.BlockSpec((rows, width), lambda i: (0, 0)),
            pl.BlockSpec((width, LAGS), lambda i: (0, 0)),
        ],
        out_specs=pl.BlockSpec((rows, block), lambda i: (0, i)),
        scratch_shapes=[pltpu.VMEM((2 * rows, width), BF16)],
        compiler_params=pltpu.CompilerParams(
            dimension_semantics=("arbitrary",), vmem_limit_bytes=12 << 20
        ),
        name="lags",
    )(x, inverse)


def local(records, pair_list, sketch):
    base, step, ibase, istep = table_parts()
    n_pair = lax.axis_size("pair")
    n_tm = lax.axis_size("tm")
    owner = lax.axis_index("pair")
    ch_dev, win_dev, _ = records.shape

    pairs = pair_list.T
    parts = np.concatenate([base, step])
    number = owner.astype(jnp.int32).reshape(1)
    (sent_a,) = whiten(records, pairs, number, parts, 0)
    shape = (n_pair, CAP) + sent_a.shape[1:]
    arrived = lax.all_to_all(sent_a.reshape(shape), "pair", 0, 0, tiled=True)
    sent_b = whiten(records, pairs, number, parts, 1)

    mine = lax.dynamic_slice_in_dim(pairs, owner * PAIRS_DEV, PAIRS_DEV, 1)
    everyone = jnp.arange(n_pair * ch_dev)
    held = jnp.any(mine.reshape(-1)[:, None] == everyone[None, :], axis=0)
    block = mine // ch_dev
    first = (block * ch_dev)[:, :, None]
    ahead = held & (everyone >= first) & (everyone < mine[:, :, None])
    rank = jnp.sum(ahead, axis=2)
    slots = (block * CAP + rank).astype(jnp.int32)
    slots_rest = ((block ^ owner) * CAP + rank).astype(jnp.int32)

    inverse, s3 = inverse_table(sketch, ibase, istep)
    blocks_a = arrived.reshape(sent_a.shape)
    blocks_a, sent_b, inverse, s3 = lax.optimization_barrier((blocks_a, sent_b, inverse, s3))
    cross_a = lax.all_to_all(correlate(slots, [blocks_a], n_tm, pltpu.HBM), "tm", 0, 0, tiled=True)
    blocks_b = [sent_b[0]] + [
        lax.ppermute(sent_b[x], "pair", [(o, o ^ x) for o in range(n_pair)])
        for x in range(1, n_pair)
    ]
    slots_rest, cross_a = lax.optimization_barrier((slots_rest, cross_a))
    cross_b = lax.all_to_all(correlate(slots_rest, blocks_b, n_tm, jax.ShapeDtypeStruct), "tm", 0, 0, tiled=True)
    stack = stack_up((cross_a, cross_b), s3, gram_excess())
    stack = lax.all_to_all(stack, "tm", 0, 0, tiled=True)
    return to_lags(stack.reshape(PAIRS_DEV, 2 * NF), inverse)


def solution(mesh):
    in_specs = (P("pair", "tm", None), P(), P())
    out_specs = P("pair", None)
    return jax.shard_map(local, mesh=mesh, in_specs=in_specs, out_specs=out_specs, check_vma=False)
```

```python
import functools
import math

import jax
import jax.numpy as jnp
import numpy as np
from jax import lax
from jax.experimental import pallas as pl
from jax.experimental.pallas import tpu as pltpu
from jax.sharding import PartitionSpec as P

SAMPLES = 2048
NF = 512
LAGS = 2048
RANK = 16
CAP = 12
PAIRS_DEV = 128
F0 = NF // 2
STEP = 32
ISTEP = 16
HALF = 8
F32 = jnp.float32
BF16 = jnp.bfloat16


def turns(first, second):
    k = np.mod(np.asarray(first)[:, None] * np.asarray(second)[None, :], SAMPLES)
    return k.astype(np.float64) * (2.0 * math.pi / SAMPLES)


def table_parts():
    freq = F0 + np.arange(NF)
    base = turns(np.arange(0, SAMPLES // 2, STEP), freq)
    step = turns(np.arange(STEP), freq)
    forward = (np.stack([np.cos(base), np.sin(base)]), np.stack([np.cos(step), np.sin(step)]))
    shifts = np.arange(LAGS) - LAGS // 2
    ibase = turns(F0 + np.arange(0, NF, ISTEP), shifts)
    istep = turns(np.arange(ISTEP), shifts)
    inverse = (
        np.stack([np.cos(ibase), np.sin(ibase)]) / math.sqrt(NF),
        np.stack([np.cos(istep), np.sin(istep)]),
    )
    return tuple(p.astype(np.float32) for p in forward + inverse)


def gram_excess():
    freq = F0 + np.arange(NF)
    shifts = np.arange(LAGS) - LAGS // 2
    angle = np.mod(freq[:, None] * shifts[None, :], SAMPLES).astype(np.float32)
    angle = angle * np.float32(2.0 * math.pi / SAMPLES)
    root = np.float32(math.sqrt(NF))
    blocks = []
    for wave in (np.cos(angle), -np.sin(angle)):
        rows = (wave / root).astype(jnp.bfloat16).astype(np.float64)
        blocks.append(rows @ rows.T - 2.0 * np.eye(NF))
    return np.stack(blocks).astype(np.float32).astype(jnp.bfloat16)


def in_hbm(x):
    return pltpu.with_memory_space_constraint(x, pltpu.HBM)


def split3(x):
    high = x.astype(BF16)
    rest = x - high.astype(F32)
    mid = rest.astype(BF16)
    low = (rest - mid.astype(F32)).astype(BF16)
    return jnp.concatenate([high, mid, low], axis=0)


def split2(x):
    high = x.astype(BF16)
    return jnp.concatenate([high, (x - high.astype(F32)).astype(BF16)], axis=0)


def sum3(x):
    n = x.shape[0] // 3
    return x[:n] + x[n : 2 * n] + x[2 * n :]


def dot_nt(a, b):
    return lax.dot_general(a, b, (((1,), (1,)), ((), ())), preferred_element_type=F32)


def dot_nn(a, b):
    return jnp.dot(a, b, preferred_element_type=F32)


def pick(pair_ref, owner, channels, peers):
    shape = (channels, PAIRS_DEV)
    column = lax.broadcasted_iota(jnp.int32, shape, 0)
    lane = lax.broadcasted_iota(jnp.int32, shape, 1)
    asked = jnp.zeros(shape, F32)
    for d in range(peers):
        named = pair_ref[:, d * PAIRS_DEV : (d + 1) * PAIRS_DEV] - owner * channels
        hit = (column == named[0:1]) | (column == named[1:2])
        seen = jnp.max(hit.astype(F32), axis=1, keepdims=True)
        asked = jnp.where(lane == d, seen, asked)
    square = (channels, channels)
    earlier = lax.broadcasted_iota(jnp.int32, square, 1) < lax.broadcasted_iota(jnp.int32, square, 0)
    before = dot_nn(earlier.astype(F32).astype(BF16), asked.astype(BF16))
    number = column.astype(F32) * asked
    rows = []
    for k in range(CAP):
        rows.append(jnp.sum(jnp.where(before == k, number, 0.0), axis=0, keepdims=True))
    return jnp.concatenate(rows, axis=0).astype(jnp.int32)


def whiten_kernel(owner_ref, pair_ref, rec_ref, parts_ref, *rest, swapped):
    peers = pair_ref.shape[1] // PAIRS_DEV
    count = peers if swapped else 1
    outs, bufs, rest = rest[:count], rest[count : 2 * count], rest[2 * count :]
    table, white, chosen, sel_ref, chosen_sem, sems = rest
    i = pl.program_id(0)
    owner = owner_ref[0]
    fetch = pltpu.make_async_copy(chosen, sel_ref, chosen_sem)

    @pl.when(i == 0)
    def _():
        chosen[...] = pick(pair_ref, owner, white.shape[0], peers)
        fetch.start()
        parity = lax.broadcasted_iota(jnp.int32, (1, NF), 1) & 1
        sign = 1.0 - 2.0 * parity.astype(F32)
        cos_step = parts_ref[2]
        sin_step = parts_ref[3]

        def body(n, carry):
            cos_base = parts_ref[0, pl.ds(n, 1), :]
            sin_base = parts_ref[1, pl.ds(n, 1), :]
            cos = cos_base * cos_step - sin_base * sin_step
            sin = sin_base * cos_step + cos_base * sin_step
            row = pl.multiple_of(n * STEP, STEP)
            far = pl.multiple_of(n * STEP + SAMPLES // 2, STEP)
            table[pl.ds(row, STEP), :NF] = cos.astype(BF16)
            table[pl.ds(row, STEP), NF:] = sin.astype(BF16)
            table[pl.ds(far, STEP), :NF] = (cos * sign).astype(BF16)
            table[pl.ds(far, STEP), NF:] = (sin * sign).astype(BF16)
            return carry

        lax.fori_loop(0, SAMPLES // 2 // STEP, body, 0)

    per, windows, samples = rec_ref.shape
    spectra = dot_nn(rec_ref[...].reshape(per * windows, samples), table[...])
    re = spectra[:, :NF]
    im = spectra[:, NF:]
    power = re * re + im * im
    level = jnp.mean(power, axis=1, keepdims=True)
    factor = lax.rsqrt(power + level + 1e-06)
    rows = jnp.concatenate([re * factor, im * factor], axis=1).astype(BF16)
    white[pl.ds(i * per, per)] = rows.reshape(per, windows, 2 * NF)

    @pl.when(i == pl.num_programs(0) - 1)
    def _():
        fetch.wait()
        sends = []
        for d in range(peers):
            buf, first = (bufs[d], 0) if swapped else (bufs[0], d * CAP)
            peer = owner ^ d if swapped else d

            def body(n, carry, buf=buf, first=first, peer=peer):
                buf[first + n] = white[sel_ref[n, peer]]
                return carry

            lax.fori_loop(0, CAP, body, 0, unroll=4)
            if swapped:
                sends.append(pltpu.make_async_copy(buf, outs[d], sems.at[d]))
            else:
                span = pl.ds(first, CAP)
                sends.append(pltpu.make_async_copy(buf.at[span], outs[0].at[span], sems.at[d]))
            sends[-1].start()
        for send in sends:
            send.wait()


def whiten(records, pairs, owner, parts, half):
    ch_dev, _, samples = records.shape
    block = 32
    peers = pairs.shape[1] // PAIRS_DEV
    if half:
        shapes = [(CAP, HALF, 2 * NF)] * peers
    else:
        shapes = [(peers * CAP, HALF, 2 * NF)]
    return pl.pallas_call(
        functools.partial(whiten_kernel, swapped=bool(half)),
        out_shape=[pltpu.HBM(shape, BF16) for shape in shapes],
        grid_spec=pltpu.PrefetchScalarGridSpec(
            num_scalar_prefetch=1,
            grid=(ch_dev // block,),
            in_specs=[
                pl.BlockSpec(pairs.shape, lambda i, owner: (0, 0)),
                pl.BlockSpec((block, HALF, samples), lambda i, owner: (i, half, 0)),
                pl.BlockSpec(parts.shape, lambda i, owner: (0, 0, 0)),
            ],
            out_specs=[pl.BlockSpec(memory_space=pltpu.HBM)] * len(shapes),
            scratch_shapes=[pltpu.VMEM(shape, BF16) for shape in shapes]
            + [
                pltpu.VMEM((samples, 2 * NF), BF16),
                pltpu.VMEM((ch_dev, HALF, 2 * NF), BF16),
                pltpu.VMEM((CAP, PAIRS_DEV), jnp.int32),
                pltpu.SMEM((CAP, PAIRS_DEV), jnp.int32),
                pltpu.SemaphoreType.DMA,
                pltpu.SemaphoreType.DMA((peers,)),
            ],
        ),
        compiler_params=pltpu.CompilerParams(
            dimension_semantics=("arbitrary",), vmem_limit_bytes=24 << 20
        ),
        name="whiten",
    )(owner, *map(in_hbm, (pairs, records, parts)))


def inverse_kernel(sketch_ref, base_ref, step_ref, inv_ref, s3_ref):
    cos_step = step_ref[0]
    sin_step = step_ref[1]

    def body(n, carry):
        cos_base = base_ref[0, pl.ds(n, 1), :]
        sin_base = base_ref[1, pl.ds(n, 1), :]
        cos = cos_base * cos_step - sin_base * sin_step
        sin = sin_base * cos_step + cos_base * sin_step
        row = pl.multiple_of(n * ISTEP, ISTEP)
        low = pl.multiple_of(n * ISTEP + NF, ISTEP)
        inv_ref[pl.ds(row, ISTEP), :] = cos.astype(BF16)
        inv_ref[pl.ds(low, ISTEP), :] = (-sin).astype(BF16)
        return carry

    lax.fori_loop(0, NF // ISTEP, body, 0)
    s3_ref[...] = split3(sum3(dot_nt(split3(sketch_ref[...]), inv_ref[...]))).astype(F32).T.astype(BF16)


def inverse_table(sketch, base, step):
    return pl.pallas_call(
        inverse_kernel,
        out_shape=(
            jax.ShapeDtypeStruct((2 * NF, LAGS), BF16),
            jax.ShapeDtypeStruct((2 * NF, 3 * RANK), BF16),
        ),
        compiler_params=pltpu.CompilerParams(vmem_limit_bytes=12 << 20),
        name="inverse_table",
    )(sketch, base, step)


def cross_kernel(slot_ref, *rest):
    if len(rest) == 2:
        arr, out_ref = rest
    else:
        blocks, (out_ref, arr) = rest[:-2], rest[-2:]

        @pl.when(pl.program_id(0) == 0)
        def _():
            size = blocks[0].shape[0]
            for n, block in enumerate(blocks):
                arr[n * size : (n + 1) * size] = block[...]

    i = pl.program_id(0)
    some, group = out_ref.shape[:2]
    bins = out_ref.shape[3] // 2

    def body(n, carry):
        at = (i * some + n) * group
        for q in range(group):
            left = arr[slot_ref[0, at + q]].astype(F32)
            right = arr[slot_ref[1, at + q]].astype(F32)
            lre, lim = left[:, :bins], left[:, bins:]
            rre, rim = right[:, :bins], right[:, bins:]
            out_ref[n, q, :, :bins] = (lre * rre + lim * rim).astype(BF16)
            out_ref[n, q, :, bins:] = (lim * rre - lre * rim).astype(BF16)
        return carry

    lax.fori_loop(0, some, body, 0)


def correlate(slots, blocks, parts, space):
    size, windows, width = blocks[0].shape
    group = PAIRS_DEV // parts
    some = 4 if parts % 4 == 0 else 1
    scratch = []
    if len(blocks) > 1:
        scratch = [pltpu.VMEM((size * len(blocks), windows, width), BF16)]
    return pl.pallas_call(
        cross_kernel,
        out_shape=space((parts, group, windows, width), BF16),
        grid_spec=pltpu.PrefetchScalarGridSpec(
            num_scalar_prefetch=1,
            grid=(parts // some,),
            in_specs=[pl.BlockSpec(blocks[0].shape, lambda i, s: (0, 0, 0))] * len(blocks),
            out_specs=pl.BlockSpec((some, group, windows, width), lambda i, s: (i, 0, 0, 0)),
            scratch_shapes=scratch,
        ),
        compiler_params=pltpu.CompilerParams(
            dimension_semantics=("arbitrary",), vmem_limit_bytes=12 << 20
        ),
        name="cross",
    )(slots, *blocks)


def gather_pair(c_ref, p):
    parts, _, windows, width = c_ref.shape
    return c_ref[:, p].reshape(parts * windows, width)


def stack_kernel(ca_ref, cb_ref, s3_ref, e_ref, o_ref, r_s, h_s, y_s, g_s, en_s):
    parts, group, windows, width = ca_ref.shape
    count = 2 * parts * windows
    s3 = s3_ref[...]
    probes = []
    for p in range(group):
        c = jnp.concatenate([gather_pair(ca_ref, p), gather_pair(cb_ref, p)], axis=0)
        probe = split3(sum3(dot_nn(c, s3).T))
        probes.append(probe)
        r_s[:, p, :] = sum3(dot_nn(probe, c))
        cf = c.astype(F32)
        en_s[pl.ds(p, 1), :] = jnp.sum(cf * cf, axis=0, keepdims=True)
    raw = r_s[...].reshape(RANK * group, width)
    raw2 = split2(raw)
    rows = RANK * group
    for half in range(2):
        lanes = slice(half * NF, (half + 1) * NF)
        more = dot_nn(raw2[:, lanes], e_ref[half])
        full = 2.0 * raw[:, lanes] + (more[:rows] + more[rows:])
        h_s[:, :, lanes] = full.reshape(RANK, group, NF)
    lane = lax.broadcasted_iota(jnp.int32, (RANK, 128), 1)
    row = lax.broadcasted_iota(jnp.int32, (RANK, 128), 0)
    unit = (lane == row + RANK).astype(F32)
    for p in range(group):
        c = jnp.concatenate([gather_pair(ca_ref, p), gather_pair(cb_ref, p)], axis=0)
        y = sum3(dot_nt(split3(h_s[:, p, :]), c))
        gram = sum3(dot_nt(split3(y), probes[p]))
        gram = gram[:, :RANK] + gram[:, RANK : 2 * RANK] + gram[:, 2 * RANK :]
        y_s[:, p, :] = y
        g_s[:, p, :] = unit
        g_s[:, p, :RANK] = gram
    ys = [y_s[r] for r in range(RANK)]
    gs = [g_s[r] for r in range(RANK)]
    for k in range(RANK):
        pivot = gs[k][:, k : k + 1]
        scale = lax.rsqrt(pivot)
        scale = scale * (1.5 - 0.5 * pivot * scale * scale)
        gs[k] = gs[k] * scale
        ys[k] = ys[k] * scale
        for r in range(k + 1, RANK):
            factor = gs[r][:, k : k + 1] * scale
            gs[r] = gs[r] - factor * gs[k]
            ys[r] = ys[r] - factor * ys[k]
    energy = jnp.sum(en_s[...], axis=1, keepdims=True)
    mix = jnp.zeros_like(gs[0])
    for r in range(RANK):
        power = jnp.sum(ys[r] * ys[r], axis=1, keepdims=True)
        total = jnp.sum(ys[r], axis=1, keepdims=True)
        gain = power / (power + energy / (2 * NF))
        mix = mix + (gain * total / count) * gs[r]
    stack = jnp.zeros((group, width), F32)
    for r in range(RANK):
        stack = stack + mix[:, RANK + r : RANK + r + 1] * r_s[r]
    for t in range(parts):
        o_ref[t] = stack.astype(BF16)


def stack_up(crosses, s3, excess):
    parts, group, windows, width = crosses[0].shape
    return pl.pallas_call(
        stack_kernel,
        out_shape=jax.ShapeDtypeStruct((parts, group, width), BF16),
        scratch_shapes=[
            pltpu.VMEM((RANK, group, width), F32),
            pltpu.VMEM((RANK, group, width), F32),
            pltpu.VMEM((RANK, group, 2 * parts * windows), F32),
            pltpu.VMEM((RANK, group, 128), F32),
            pltpu.VMEM((group, width), F32),
        ],
        compiler_params=pltpu.CompilerParams(vmem_limit_bytes=24 << 20),
        name="stack",
    )(*crosses, s3, excess)


def lags_kernel(x_ref, inv_ref, o_ref):
    block = o_ref.shape[1]
    at = pl.multiple_of(pl.program_id(0) * block, block)
    o_ref[...] = dot_nn(x_ref[...], inv_ref[:, pl.ds(at, block)])


def to_lags(x, inverse):
    rows, width = x.shape
    block = 512
    return pl.pallas_call(
        lags_kernel,
        out_shape=jax.ShapeDtypeStruct((rows, LAGS), F32),
        grid=(LAGS // block,),
        in_specs=[
            pl.BlockSpec((rows, width), lambda i: (0, 0)),
            pl.BlockSpec((width, LAGS), lambda i: (0, 0)),
        ],
        out_specs=pl.BlockSpec((rows, block), lambda i: (0, i)),
        compiler_params=pltpu.CompilerParams(
            dimension_semantics=("arbitrary",), vmem_limit_bytes=12 << 20
        ),
        name="lags",
    )(x, inverse)


def local(records, pair_list, sketch):
    base, step, ibase, istep = table_parts()
    n_pair = lax.axis_size("pair")
    n_tm = lax.axis_size("tm")
    owner = lax.axis_index("pair")
    ch_dev, win_dev, _ = records.shape

    pairs = pair_list.T
    parts = np.concatenate([base, step])
    number = owner.astype(jnp.int32).reshape(1)
    (sent_a,) = whiten(records, pairs, number, parts, 0)
    shape = (n_pair, CAP) + sent_a.shape[1:]
    arrived = lax.all_to_all(sent_a.reshape(shape), "pair", 0, 0, tiled=True)
    sent_b = whiten(records, pairs, number, parts, 1)

    mine = lax.dynamic_slice_in_dim(pairs, owner * PAIRS_DEV, PAIRS_DEV, 1)
    everyone = jnp.arange(n_pair * ch_dev)
    held = jnp.any(mine.reshape(-1)[:, None] == everyone[None, :], axis=0)
    block = mine // ch_dev
    first = (block * ch_dev)[:, :, None]
    ahead = held & (everyone >= first) & (everyone < mine[:, :, None])
    rank = jnp.sum(ahead, axis=2)
    slots = (block * CAP + rank).astype(jnp.int32)
    slots_rest = ((block ^ owner) * CAP + rank).astype(jnp.int32)

    inverse, s3 = inverse_table(sketch, ibase, istep)
    blocks_a = arrived.reshape(sent_a.shape)
    blocks_a, sent_b, inverse, s3 = lax.optimization_barrier((blocks_a, sent_b, inverse, s3))
    cross_a = lax.all_to_all(correlate(slots, [blocks_a], n_tm, pltpu.HBM), "tm", 0, 0, tiled=True)
    blocks_b = [sent_b[0]] + [
        lax.ppermute(sent_b[x], "pair", [(o, o ^ x) for o in range(n_pair)])
        for x in range(1, n_pair)
    ]
    slots_rest, cross_a = lax.optimization_barrier((slots_rest, cross_a))
    cross_b = lax.all_to_all(correlate(slots_rest, blocks_b, n_tm, jax.ShapeDtypeStruct), "tm", 0, 0, tiled=True)
    stack = stack_up((cross_a, cross_b), s3, gram_excess())
    stack = lax.all_to_all(stack, "tm", 0, 0, tiled=True)
    return to_lags(stack.reshape(PAIRS_DEV, 2 * NF), inverse)


def solution(mesh):
    in_specs = (P("pair", "tm", None), P(), P())
    out_specs = P("pair", None)
    return jax.shard_map(local, mesh=mesh, in_specs=in_specs, out_specs=out_specs, check_vma=False)
```

```python
import functools
import math

import jax
import jax.numpy as jnp
import numpy as np
from jax import lax
from jax.experimental import pallas as pl
from jax.experimental.pallas import tpu as pltpu
from jax.sharding import PartitionSpec as P

SAMPLES = 2048
NF = 512
LAGS = 2048
RANK = 16
CAP = 12
PAIRS_DEV = 128
F0 = NF // 2
STEP = 32
ISTEP = 16
HALF = 8
F32 = jnp.float32
BF16 = jnp.bfloat16


def turns(first, second):
    k = np.mod(np.asarray(first)[:, None] * np.asarray(second)[None, :], SAMPLES)
    return k.astype(np.float64) * (2.0 * math.pi / SAMPLES)


def table_parts():
    freq = F0 + np.arange(NF)
    base = turns(np.arange(0, SAMPLES // 2, STEP), freq)
    step = turns(np.arange(STEP), freq)
    forward = (np.stack([np.cos(base), np.sin(base)]), np.stack([np.cos(step), np.sin(step)]))
    shifts = np.arange(LAGS) - LAGS // 2
    ibase = turns(F0 + np.arange(0, NF, ISTEP), shifts)
    istep = turns(np.arange(ISTEP), shifts)
    inverse = (
        np.stack([np.cos(ibase), np.sin(ibase)]) / math.sqrt(NF),
        np.stack([np.cos(istep), np.sin(istep)]),
    )
    return tuple(p.astype(np.float32) for p in forward + inverse)


def gram_excess():
    freq = F0 + np.arange(NF)
    shifts = np.arange(LAGS) - LAGS // 2
    angle = np.mod(freq[:, None] * shifts[None, :], SAMPLES).astype(np.float32)
    angle = angle * np.float32(2.0 * math.pi / SAMPLES)
    root = np.float32(math.sqrt(NF))
    blocks = []
    for wave in (np.cos(angle), -np.sin(angle)):
        rows = (wave / root).astype(jnp.bfloat16).astype(np.float64)
        blocks.append(rows @ rows.T - 2.0 * np.eye(NF))
    return np.stack(blocks).astype(np.float32).astype(jnp.bfloat16)


def in_hbm(x):
    return pltpu.with_memory_space_constraint(x, pltpu.HBM)


def split3(x):
    high = x.astype(BF16)
    rest = x - high.astype(F32)
    mid = rest.astype(BF16)
    low = (rest - mid.astype(F32)).astype(BF16)
    return jnp.concatenate([high, mid, low], axis=0)


def split2(x):
    high = x.astype(BF16)
    return jnp.concatenate([high, (x - high.astype(F32)).astype(BF16)], axis=0)


def sum3(x):
    n = x.shape[0] // 3
    return x[:n] + x[n : 2 * n] + x[2 * n :]


def dot_nt(a, b):
    return lax.dot_general(a, b, (((1,), (1,)), ((), ())), preferred_element_type=F32)


def dot_nn(a, b):
    return jnp.dot(a, b, preferred_element_type=F32)


def pick(pair_ref, owner, channels, peers):
    shape = (channels, PAIRS_DEV)
    column = lax.broadcasted_iota(jnp.int32, shape, 0)
    lane = lax.broadcasted_iota(jnp.int32, shape, 1)
    asked = jnp.zeros(shape, F32)
    for d in range(peers):
        named = pair_ref[:, d * PAIRS_DEV : (d + 1) * PAIRS_DEV] - owner * channels
        hit = (column == named[0:1]) | (column == named[1:2])
        seen = jnp.max(hit.astype(F32), axis=1, keepdims=True)
        asked = jnp.where(lane == d, seen, asked)
    square = (channels, channels)
    earlier = lax.broadcasted_iota(jnp.int32, square, 1) < lax.broadcasted_iota(jnp.int32, square, 0)
    before = dot_nn(earlier.astype(F32).astype(BF16), asked.astype(BF16))
    number = column.astype(F32) * asked
    rows = []
    for k in range(CAP):
        rows.append(jnp.sum(jnp.where(before == k, number, 0.0), axis=0, keepdims=True))
    return jnp.concatenate(rows, axis=0).astype(jnp.int32)


def whiten_kernel(owner_ref, pair_ref, rec_ref, parts_ref, *rest, swapped):
    peers = pair_ref.shape[1] // PAIRS_DEV
    count = peers if swapped else 1
    outs, bufs, rest = rest[:count], rest[count : 2 * count], rest[2 * count :]
    table, white, chosen, sel_ref, chosen_sem, sems = rest
    i = pl.program_id(0)
    owner = owner_ref[0]
    fetch = pltpu.make_async_copy(chosen, sel_ref, chosen_sem)

    @pl.when(i == 0)
    def _():
        chosen[...] = pick(pair_ref, owner, white.shape[0], peers)
        fetch.start()
        parity = lax.broadcasted_iota(jnp.int32, (1, NF), 1) & 1
        sign = 1.0 - 2.0 * parity.astype(F32)
        cos_step = parts_ref[2]
        sin_step = parts_ref[3]

        def body(n, carry):
            cos_base = parts_ref[0, pl.ds(n, 1), :]
            sin_base = parts_ref[1, pl.ds(n, 1), :]
            cos = cos_base * cos_step - sin_base * sin_step
            sin = sin_base * cos_step + cos_base * sin_step
            row = pl.multiple_of(n * STEP, STEP)
            far = pl.multiple_of(n * STEP + SAMPLES // 2, STEP)
            table[pl.ds(row, STEP), :NF] = cos.astype(BF16)
            table[pl.ds(row, STEP), NF:] = sin.astype(BF16)
            table[pl.ds(far, STEP), :NF] = (cos * sign).astype(BF16)
            table[pl.ds(far, STEP), NF:] = (sin * sign).astype(BF16)
            return carry

        lax.fori_loop(0, SAMPLES // 2 // STEP, body, 0)

    per, windows, samples = rec_ref.shape
    spectra = dot_nn(rec_ref[...].reshape(per * windows, samples), table[...])
    re = spectra[:, :NF]
    im = spectra[:, NF:]
    power = re * re + im * im
    level = jnp.mean(power, axis=1, keepdims=True)
    factor = lax.rsqrt(power + level + 1e-06)
    rows = jnp.concatenate([re * factor, im * factor], axis=1).astype(BF16)
    white[pl.ds(i * per, per)] = rows.reshape(per, windows, 2 * NF)

    @pl.when(i == pl.num_programs(0) - 1)
    def _():
        fetch.wait()
        sends = []
        for d in range(peers):
            buf, first = (bufs[d], 0) if swapped else (bufs[0], d * CAP)
            peer = owner ^ d if swapped else d

            def body(n, carry, buf=buf, first=first, peer=peer):
                buf[first + n] = white[sel_ref[n, peer]]
                return carry

            lax.fori_loop(0, CAP, body, 0, unroll=4)
            if swapped:
                sends.append(pltpu.make_async_copy(buf, outs[d], sems.at[d]))
            else:
                span = pl.ds(first, CAP)
                sends.append(pltpu.make_async_copy(buf.at[span], outs[0].at[span], sems.at[d]))
            sends[-1].start()
        for send in sends:
            send.wait()


def whiten(records, pairs, owner, parts, half):
    ch_dev, _, samples = records.shape
    block = 32
    peers = pairs.shape[1] // PAIRS_DEV
    if half:
        shapes = [(CAP, HALF, 2 * NF)] * peers
    else:
        shapes = [(peers * CAP, HALF, 2 * NF)]
    return pl.pallas_call(
        functools.partial(whiten_kernel, swapped=bool(half)),
        out_shape=[pltpu.HBM(shape, BF16) for shape in shapes],
        grid_spec=pltpu.PrefetchScalarGridSpec(
            num_scalar_prefetch=1,
            grid=(ch_dev // block,),
            in_specs=[
                pl.BlockSpec(pairs.shape, lambda i, owner: (0, 0)),
                pl.BlockSpec((block, HALF, samples), lambda i, owner: (i, half, 0)),
                pl.BlockSpec(parts.shape, lambda i, owner: (0, 0, 0)),
            ],
            out_specs=[pl.BlockSpec(memory_space=pltpu.HBM)] * len(shapes),
            scratch_shapes=[pltpu.VMEM(shape, BF16) for shape in shapes]
            + [
                pltpu.VMEM((samples, 2 * NF), BF16),
                pltpu.VMEM((ch_dev, HALF, 2 * NF), BF16),
                pltpu.VMEM((CAP, PAIRS_DEV), jnp.int32),
                pltpu.SMEM((CAP, PAIRS_DEV), jnp.int32),
                pltpu.SemaphoreType.DMA,
                pltpu.SemaphoreType.DMA((peers,)),
            ],
        ),
        compiler_params=pltpu.CompilerParams(
            dimension_semantics=("arbitrary",), vmem_limit_bytes=24 << 20
        ),
        name="whiten",
    )(owner, *map(in_hbm, (pairs, records, parts)))


def inverse_kernel(sketch_ref, base_ref, step_ref, inv_ref, s3_ref):
    cos_step = step_ref[0]
    sin_step = step_ref[1]

    def body(n, carry):
        cos_base = base_ref[0, pl.ds(n, 1), :]
        sin_base = base_ref[1, pl.ds(n, 1), :]
        cos = cos_base * cos_step - sin_base * sin_step
        sin = sin_base * cos_step + cos_base * sin_step
        row = pl.multiple_of(n * ISTEP, ISTEP)
        low = pl.multiple_of(n * ISTEP + NF, ISTEP)
        inv_ref[pl.ds(row, ISTEP), :] = cos.astype(BF16)
        inv_ref[pl.ds(low, ISTEP), :] = (-sin).astype(BF16)
        return carry

    lax.fori_loop(0, NF // ISTEP, body, 0)
    s3_ref[...] = split3(sum3(dot_nt(split3(sketch_ref[...]), inv_ref[...]))).astype(F32).T.astype(BF16)


def inverse_table(sketch, base, step):
    return pl.pallas_call(
        inverse_kernel,
        out_shape=(
            jax.ShapeDtypeStruct((2 * NF, LAGS), BF16),
            jax.ShapeDtypeStruct((2 * NF, 3 * RANK), BF16),
        ),
        compiler_params=pltpu.CompilerParams(vmem_limit_bytes=12 << 20),
        name="inverse_table",
    )(sketch, base, step)


def cross_kernel(slot_ref, *rest):
    if len(rest) == 2:
        arr, out_ref = rest
    else:
        blocks, (out_ref, arr) = rest[:-2], rest[-2:]

        @pl.when(pl.program_id(0) == 0)
        def _():
            size = blocks[0].shape[0]
            for n, block in enumerate(blocks):
                arr[n * size : (n + 1) * size] = block[...]

    i = pl.program_id(0)
    some, group = out_ref.shape[:2]
    bins = out_ref.shape[3] // 2

    def body(n, carry):
        at = (i * some + n) * group
        for q in range(group):
            left = arr[slot_ref[0, at + q]].astype(F32)
            right = arr[slot_ref[1, at + q]].astype(F32)
            lre, lim = left[:, :bins], left[:, bins:]
            rre, rim = right[:, :bins], right[:, bins:]
            out_ref[n, q, :, :bins] = (lre * rre + lim * rim).astype(BF16)
            out_ref[n, q, :, bins:] = (lim * rre - lre * rim).astype(BF16)
        return carry

    lax.fori_loop(0, some, body, 0)


def correlate(slots, blocks, parts, space):
    size, windows, width = blocks[0].shape
    group = PAIRS_DEV // parts
    some = 4 if parts % 4 == 0 else 1
    scratch = []
    if len(blocks) > 1:
        scratch = [pltpu.VMEM((size * len(blocks), windows, width), BF16)]
    return pl.pallas_call(
        cross_kernel,
        out_shape=space((parts, group, windows, width), BF16),
        grid_spec=pltpu.PrefetchScalarGridSpec(
            num_scalar_prefetch=1,
            grid=(parts // some,),
            in_specs=[pl.BlockSpec(blocks[0].shape, lambda i, s: (0, 0, 0))] * len(blocks),
            out_specs=pl.BlockSpec((some, group, windows, width), lambda i, s: (i, 0, 0, 0)),
            scratch_shapes=scratch,
        ),
        compiler_params=pltpu.CompilerParams(
            dimension_semantics=("arbitrary",), vmem_limit_bytes=12 << 20
        ),
        name="cross",
    )(slots, *blocks)


def gather_pair(c_ref, p):
    parts, _, windows, width = c_ref.shape
    return c_ref[:, p].reshape(parts * windows, width)


def stack_kernel(ca_ref, cb_ref, s3_ref, e_ref, o_ref, r_s, h_s, y_s, g_s, en_s):
    parts, group, windows, width = ca_ref.shape
    count = 2 * parts * windows
    s3 = s3_ref[...]
    probes = []
    for p in range(group):
        c = jnp.concatenate([gather_pair(ca_ref, p), gather_pair(cb_ref, p)], axis=0)
        probe = split3(sum3(dot_nn(c, s3).T))
        probes.append(probe)
        r_s[:, p, :] = sum3(dot_nn(probe, c))
        cf = c.astype(F32)
        en_s[pl.ds(p, 1), :] = jnp.sum(cf * cf, axis=0, keepdims=True)
    raw = r_s[...].reshape(RANK * group, width)
    raw2 = split2(raw)
    rows = RANK * group
    for half in range(2):
        lanes = slice(half * NF, (half + 1) * NF)
        more = dot_nn(raw2[:, lanes], e_ref[half])
        full = 2.0 * raw[:, lanes] + (more[:rows] + more[rows:])
        h_s[:, :, lanes] = full.reshape(RANK, group, NF)
    lane = lax.broadcasted_iota(jnp.int32, (RANK, 128), 1)
    row = lax.broadcasted_iota(jnp.int32, (RANK, 128), 0)
    unit = (lane == row + RANK).astype(F32)
    for p in range(group):
        c = jnp.concatenate([gather_pair(ca_ref, p), gather_pair(cb_ref, p)], axis=0)
        y = sum3(dot_nt(split3(h_s[:, p, :]), c))
        gram = sum3(dot_nt(split3(y), probes[p]))
        gram = gram[:, :RANK] + gram[:, RANK : 2 * RANK] + gram[:, 2 * RANK :]
        y_s[:, p, :] = y
        g_s[:, p, :] = unit
        g_s[:, p, :RANK] = gram
    ys = [y_s[r] for r in range(RANK)]
    gs = [g_s[r] for r in range(RANK)]
    for k in range(RANK):
        pivot = gs[k][:, k : k + 1]
        scale = lax.rsqrt(pivot)
        scale = scale * (1.5 - 0.5 * pivot * scale * scale)
        gs[k] = gs[k] * scale
        ys[k] = ys[k] * scale
        for r in range(k + 1, RANK):
            factor = gs[r][:, k : k + 1] * scale
            gs[r] = gs[r] - factor * gs[k]
            ys[r] = ys[r] - factor * ys[k]
    energy = jnp.sum(en_s[...], axis=1, keepdims=True)
    mix = jnp.zeros_like(gs[0])
    for r in range(RANK):
        power = jnp.sum(ys[r] * ys[r], axis=1, keepdims=True)
        total = jnp.sum(ys[r], axis=1, keepdims=True)
        gain = power / (power + energy / (2 * NF))
        mix = mix + (gain * total / count) * gs[r]
    stack = jnp.zeros((group, width), F32)
    for r in range(RANK):
        stack = stack + mix[:, RANK + r : RANK + r + 1] * r_s[r]
    for t in range(parts):
        o_ref[t] = stack.astype(BF16)


def stack_up(crosses, s3, excess):
    parts, group, windows, width = crosses[0].shape
    return pl.pallas_call(
        stack_kernel,
        out_shape=jax.ShapeDtypeStruct((parts, group, width), BF16),
        scratch_shapes=[
            pltpu.VMEM((RANK, group, width), F32),
            pltpu.VMEM((RANK, group, width), F32),
            pltpu.VMEM((RANK, group, 2 * parts * windows), F32),
            pltpu.VMEM((RANK, group, 128), F32),
            pltpu.VMEM((group, width), F32),
        ],
        compiler_params=pltpu.CompilerParams(vmem_limit_bytes=24 << 20),
        name="stack",
    )(*crosses, s3, excess)


def lags_kernel(x_ref, inv_ref, o_ref):
    block = o_ref.shape[1]
    at = pl.multiple_of(pl.program_id(0) * block, block)
    o_ref[...] = dot_nn(x_ref[...], inv_ref[:, pl.ds(at, block)])


def to_lags(x, inverse):
    rows, width = x.shape
    block = 1024
    return pl.pallas_call(
        lags_kernel,
        out_shape=jax.ShapeDtypeStruct((rows, LAGS), F32),
        grid=(LAGS // block,),
        in_specs=[
            pl.BlockSpec((rows, width), lambda i: (0, 0)),
            pl.BlockSpec((width, LAGS), lambda i: (0, 0)),
        ],
        out_specs=pl.BlockSpec((rows, block), lambda i: (0, i)),
        compiler_params=pltpu.CompilerParams(
            dimension_semantics=("arbitrary",), vmem_limit_bytes=12 << 20
        ),
        name="lags",
    )(x, inverse)


def local(records, pair_list, sketch):
    base, step, ibase, istep = table_parts()
    n_pair = lax.axis_size("pair")
    n_tm = lax.axis_size("tm")
    owner = lax.axis_index("pair")
    ch_dev, win_dev, _ = records.shape

    pairs = pair_list.T
    parts = np.concatenate([base, step])
    number = owner.astype(jnp.int32).reshape(1)
    (sent_a,) = whiten(records, pairs, number, parts, 0)
    shape = (n_pair, CAP) + sent_a.shape[1:]
    arrived = lax.all_to_all(sent_a.reshape(shape), "pair", 0, 0, tiled=True)
    sent_b = whiten(records, pairs, number, parts, 1)

    mine = lax.dynamic_slice_in_dim(pairs, owner * PAIRS_DEV, PAIRS_DEV, 1)
    everyone = jnp.arange(n_pair * ch_dev)
    held = jnp.any(mine.reshape(-1)[:, None] == everyone[None, :], axis=0)
    block = mine // ch_dev
    first = (block * ch_dev)[:, :, None]
    ahead = held & (everyone >= first) & (everyone < mine[:, :, None])
    rank = jnp.sum(ahead, axis=2)
    slots = (block * CAP + rank).astype(jnp.int32)
    slots_rest = ((block ^ owner) * CAP + rank).astype(jnp.int32)

    inverse, s3 = inverse_table(sketch, ibase, istep)
    blocks_a = arrived.reshape(sent_a.shape)
    blocks_a, sent_b, inverse, s3 = lax.optimization_barrier((blocks_a, sent_b, inverse, s3))
    cross_a = lax.all_to_all(correlate(slots, [blocks_a], n_tm, pltpu.HBM), "tm", 0, 0, tiled=True)
    blocks_b = [sent_b[0]] + [
        lax.ppermute(sent_b[x], "pair", [(o, o ^ x) for o in range(n_pair)])
        for x in range(1, n_pair)
    ]
    slots_rest, cross_a = lax.optimization_barrier((slots_rest, cross_a))
    cross_b = lax.all_to_all(correlate(slots_rest, blocks_b, n_tm, jax.ShapeDtypeStruct), "tm", 0, 0, tiled=True)
    stack = stack_up((cross_a, cross_b), s3, gram_excess())
    stack = lax.all_to_all(stack, "tm", 0, 0, tiled=True)
    return to_lags(stack.reshape(PAIRS_DEV, 2 * NF), inverse)


def solution(mesh):
    in_specs = (P("pair", "tm", None), P(), P())
    out_specs = P("pair", None)
    return jax.shard_map(local, mesh=mesh, in_specs=in_specs, out_specs=out_specs, check_vma=False)
```
